1024 devices in a mesh: tile: 128 (over x, z, core), batch: 8 (over y).
Axes of the slice: x: 4, y: 8, z: 16, core: 2. Of those that a mesh axis runs over, the one named last changes fastest.
Arguments:
- object_slices: float32 [128, 2, 2, 256, 256], P('tile'), may hold values from -1 to 1
- probe: float32 [2, 2, 128, 128], replicated, may hold values from -6 to 6
- prop_phase: float32 [128, 128], replicated, may hold values from -3.140625 to 3.140625
- scan_offsets: int32 [128, 8, 2], P('tile', 'batch'), may hold values from 0 to 255, as said below
- measured: float32 [128, 8, 128, 128], P('tile', 'batch'), may hold values from 0 to 2
Outputs:
- object_grad: float32 [128, 2, 2, 256, 256], P('tile', None, None, 'batch')
- probe_step: float32 [2, 2, 128, 128], replicated
The draws below stay inside these ranges and needn't reach their ends.
Inputs may be any that keep to these rules, and one draw needn't show every extreme that they name: `scan_offsets`: offsets are relative to the tile that holds the position. A window never leaves the object: in the last row of the tile grid the row offset is at most 128, in the last column of the tile grid the column offset is at most 128.
All inputs are finite; a program needn't handle non-finite values.
Results may differ from the reference program's by a relative error of at most 0.00012.
Values sent between devices are 32-bit elements; how exact they have to be, the bound alone decides.
A program may use at most 32 MiB of HBM per device.

```python
import math
import jax
import jax.numpy as jnp
from jax import lax

W = 128
MODES = 2
NSL = 2
TS = 256
TGX = 8
TILES = 128
TGY = 16
SLOTS = 8
POSITIONS = 1024


def draw_scan_offsets(key, part):
    tile_index = jnp.arange(TILES, dtype=jnp.int32)
    grid_rows = TILES // TGX
    row_limit = jnp.where(tile_index // TGX < grid_rows - 1, TS, TS - W + 1)
    col_limit = jnp.where(tile_index % TGX < TGX - 1, TS, TS - W + 1)
    limits = jnp.stack([row_limit, col_limit], axis=1)[:, None, :]
    values = jax.random.randint(key, (TILES, SLOTS, 2), 0, limits, dtype=jnp.int32)
    values = values.at[0, 0, 0].set(0).at[0, 0, 1].set(TS - 1)
    return values


def block_levels(own_key, shape, cuts, smallest, high):
    gain, own = 1.0, jax.random.fold_in(own_key, 6)
    for position, parts in cuts:
        draws = jnp.exp(jax.random.uniform(jax.random.fold_in(own, position), (parts,), jnp.float32, smallest / len(cuts), high / len(cuts)))
        gain = gain * jnp.repeat(draws, shape[position] // parts).reshape([-1 if axis == position else 1 for axis in range(len(shape))])
    return gain


def normal_values(own_key, dims, scale, bound, kind=jnp.bfloat16):
    drawn = scale * jax.random.normal(own_key, dims, jnp.float32)
    return jnp.clip(drawn, min=-bound, max=bound).astype(kind)


def setup_inputs(seed: int = 0) -> dict:
    seeds = jax.random.split(jax.random.key(seed), 6)
    object_slices = jnp.clip(jax.random.uniform(seeds[0], (TILES, NSL, 2, TS, TS), jnp.float32, -1.0, 1.0) * block_levels(seeds[0], (TILES, NSL, 2, TS, TS), ((0, 128),), -0.4, 0.0), -1.0, 1.0)
    probe = normal_values(seeds[1], (MODES, 2, W, W), 1.0, 6.0, jnp.float32)
    prop_phase = jnp.clip(jax.random.uniform(seeds[2], (W, W), jnp.float32, -3.140625, 3.140625), -3.140625, 3.140625)
    scan_offsets = draw_scan_offsets(jax.random.fold_in(seeds[5], 71), 0)
    measured = jnp.clip(2.0 * jax.random.uniform(seeds[4], (TILES, SLOTS, W, W), jnp.float32) ** block_levels(seeds[4], (TILES, SLOTS, W, W), ((0, 128), (1, 8)), -0.2, 0.2), 0.0, 2.0)
    return {"object_slices": object_slices, "probe": probe, "prop_phase": prop_phase, "scan_offsets": scan_offsets, "measured": measured}


LOSS_SCALE = 0.05

def fourier_tables(extent):
    indices = jnp.arange(extent, dtype=jnp.int32)
    phases = (indices[:, None] * indices[None, :] % extent).astype(jnp.float32) * (2.0 * math.pi / extent)
    scaling = 1.0 / math.sqrt(extent)
    return (jnp.cos(phases) * scaling, -jnp.sin(phases) * scaling)

def complex_product(left_op, right_op):
    return (left_op[0] * right_op[0] - left_op[1] * right_op[1], left_op[0] * right_op[1] + left_op[1] * right_op[0])

def transform(fields, table_real, table_imag):
    highest = lax.Precision.HIGHEST
    left_real = jnp.einsum('jk,bkl->bjl', table_real, fields[0], precision=highest) - jnp.einsum('jk,bkl->bjl', table_imag, fields[1], precision=highest)
    left_imag = jnp.einsum('jk,bkl->bjl', table_real, fields[1], precision=highest) + jnp.einsum('jk,bkl->bjl', table_imag, fields[0], precision=highest)
    out_real = jnp.einsum('bjk,kl->bjl', left_real, table_real, precision=highest) - jnp.einsum('bjk,kl->bjl', left_imag, table_imag, precision=highest)
    out_imag = jnp.einsum('bjk,kl->bjl', left_real, table_imag, precision=highest) + jnp.einsum('bjk,kl->bjl', left_imag, table_real, precision=highest)
    return (out_real, out_imag)

def window_loss(windows, probe, prop_real, prop_imag, target):
    positions = windows.shape[0]
    layers = windows.shape[1]
    mode_count = probe.shape[0]
    extent = probe.shape[-1]
    table_real, table_imag = fourier_tables(extent)
    shape_full = (positions, mode_count, extent, extent)
    shape_flat = (positions * mode_count, extent, extent)
    wavefield = (jnp.broadcast_to(probe[None, :, 0], shape_full), jnp.broadcast_to(probe[None, :, 1], shape_full))
    for slab_index in range(layers):
        if slab_index > 0:
            flattened = (wavefield[0].reshape(shape_flat), wavefield[1].reshape(shape_flat))
            spectrum = complex_product(transform(flattened, table_real, table_imag), (prop_real, prop_imag))
            flattened = transform(spectrum, table_real, -table_imag)
            wavefield = (flattened[0].reshape(shape_full), flattened[1].reshape(shape_full))
        slab_now = (windows[:, slab_index, 0][:, None], windows[:, slab_index, 1][:, None])
        wavefield = complex_product(wavefield, slab_now)
    far_field = transform((wavefield[0].reshape(shape_flat), wavefield[1].reshape(shape_flat)), table_real, table_imag)
    intensity = lax.optimization_barrier(jnp.sum((far_field[0] * far_field[0] + far_field[1] * far_field[1]).reshape(shape_full), axis=1))
    return LOSS_SCALE * jnp.sum((intensity - target) ** 2)

def reference(object_slices, probe, prop_phase, scan_offsets, measured):
    prop_real = jnp.cos(prop_phase)
    prop_imag = jnp.sin(prop_phase)
    frame = object_slices.reshape(TGY, TGX, NSL, 2, TS, TS).transpose(2, 3, 0, 4, 1, 5).reshape(NSL, 2, TGY * TS, TGX * TS)
    tile_index = jnp.arange(TILES, dtype=jnp.int32)
    row_anchor = (tile_index // TGX * TS)[:, None] + scan_offsets[:, :, 0]
    col_anchor = (tile_index % TGX * TS)[:, None] + scan_offsets[:, :, 1]
    zero_index = jnp.zeros((), jnp.int32)

    def cut_window(row_at, col_at):
        return lax.dynamic_slice(frame, (zero_index, zero_index, row_at, col_at), (NSL, 2, W, W))

    def per_tile(carry, inputs):
        grad_frame, probe_total = carry
        rows_here, cols_here, target = inputs
        windows = jax.vmap(cut_window)(rows_here, cols_here)
        window_grad, probe_grad = jax.grad(window_loss, argnums=(0, 1))(windows, probe, prop_real, prop_imag, target)

        def add_window(slot_index, frame_accum):
            start = (zero_index, zero_index, rows_here[slot_index], cols_here[slot_index])
            current = lax.dynamic_slice(frame_accum, start, (NSL, 2, W, W))
            return lax.dynamic_update_slice(frame_accum, current + window_grad[slot_index], start)
        grad_frame = lax.fori_loop(0, SLOTS, add_window, grad_frame)
        return ((grad_frame, probe_total + probe_grad), None)
    initial = (jnp.zeros(frame.shape, jnp.float32), jnp.zeros(probe.shape, jnp.float32))
    (grad_frame, probe_total), _ = lax.scan(per_tile, initial, (row_anchor, col_anchor, measured))
    object_grad = grad_frame.reshape(NSL, 2, TGY, TS, TGX, TS).transpose(2, 4, 0, 1, 3, 5).reshape(TILES, NSL, 2, TS, TS)
    return (object_grad, probe_total / POSITIONS)
```

```python
import functools
import math

import jax
import jax.numpy as jnp
import ml_dtypes
import numpy as np
from jax import lax
from jax.experimental import pallas as pl
from jax.experimental.pallas import tpu as pltpu
from jax.sharding import PartitionSpec as P

TGX = 8
XS = 4
LOSS_SCALE = 0.05
W = 128
F32 = jnp.float32
BF16 = jnp.bfloat16
MESH = pl.DeviceIdType.MESH


def table_parts():
    idx = np.arange(W)
    phase = (idx[:, None] * idx[None, :] % W) * (2.0 * math.pi / W)
    c, s = np.cos(phase) / math.sqrt(W), -np.sin(phase) / math.sqrt(W)
    left = np.block([[c, -s], [s, c]]).astype(np.float32)
    right = np.block([[c, s], [-s, c]]).astype(np.float32)

    def parts(m):
        hi = m.astype(ml_dtypes.bfloat16)
        return hi, (m - hi.astype(np.float32)).astype(ml_dtypes.bfloat16)

    lh, ll = parts(left)
    rh, rl = parts(right)
    by_rows = [np.concatenate([h, h, l], 0) for h, l in ((lh, ll), (rh, rl))]
    by_cols = [np.concatenate([h, l, h], 1) for h, l in ((lh, ll), (rh, rl))]
    return np.stack(by_rows), np.stack(by_cols)


def split(d):
    hi = d.astype(BF16)
    return hi, (d - hi.astype(F32)).astype(BF16)


def from_right(d, table):
    hi, lo = split(d)
    return jnp.dot(jnp.concatenate([hi, lo, hi], 1), table, preferred_element_type=F32)


def from_left(d, table):
    hi, lo = split(d)
    return jnp.dot(table, jnp.concatenate([hi, hi, lo], 0), preferred_element_type=F32)


def swap_blocks(d):
    top = jnp.concatenate([d[:W, :W], d[W:, :W]], 1)
    low = jnp.concatenate([d[:W, W:], d[W:, W:]], 1)
    return jnp.concatenate([top, low], 0)


def kernel(
    geo,
    offs_ref, obj, probe, phase, meas, trow_h, tcol_h,
    out_g, out_p,
    ext, win, prb, hph, msr, trow, tcol, mid, offs, sel,
    gwin, gbuf, acc, r_right, r_low, r_diag, fin, r_fin,
    pg, p_core, s_core, p_x, s_x, p_y, p_z, pout,
    loc_sem, f1_s, f1_r, of_s, of_r, f2_s, f2_r, g1_s, g1_r, g2_s, g2_r, g3_s, g3_r,
    pc_s, pc_r, px_s, px_r, py_s, py_r, pz_s, pz_r, qy_s, qy_r, qx_s, qx_r, qc_s, qc_r,
):
    X, Z, NB, tgx = geo
    T = X * Z * 2
    RC = W // NB
    XP = 2 * W // X
    YP = XP // NB
    half = NB // 2
    t = lax.axis_index("tile")
    j = lax.axis_index("batch")
    core = lax.rem(t, 2)
    z = lax.rem(t // 2, Z)
    x = t // (2 * Z)
    sib = t + 1 - 2 * core

    def z_tile(d):
        return (x * Z + lax.rem(z + d, Z)) * 2 + core

    def x_tile(d):
        return (lax.rem(x + d, X) * Z + z) * 2 + core

    def y_dev(d):
        return lax.rem(j + d, NB)

    def cls(dev):
        return 2 * lax.rem(dev, half) + dev // half

    def rows_of(dev):
        return pl.ds(pl.multiple_of(RC * cls(dev), RC), RC)

    near = (1, tgx, tgx + 1)

    barrier = pltpu.get_barrier_semaphore()

    def greet(tile, dev):
        pl.semaphore_signal(barrier, inc=1, device_id=(tile, dev), device_id_type=MESH)

    for n in near:
        greet(lax.rem(t + n, T), j)
        greet(lax.rem(t + T - n, T), j)
    greet(sib, j)
    lax.fori_loop(1, NB, lambda d, c: (greet(t, y_dev(d)), c)[1], 0)
    lax.fori_loop(1, X, lambda d, c: (greet(x_tile(d), j), c)[1], 0)
    lax.fori_loop(1, Z, lambda d, c: (greet(z_tile(d), j), c)[1], 0)

    mine = rows_of(j)
    local = [
        pltpu.make_async_copy(obj.at[l, :, :, mine, :], ext.at[l, :, 0:2, :, 0 : 2 * W], loc_sem.at[l])
        for l in range(2)
    ] + [
        pltpu.make_async_copy(a, b, loc_sem.at[2 + i])
        for i, (a, b) in enumerate(((probe, prb), (phase, hph.at[0]), (meas, msr), (trow_h, trow), (tcol_h, tcol)))
    ]
    for c in local:
        c.start()

    row_off = offs_ref[0]
    col_off = offs_ref[1]
    offs[j, 0] = jnp.full((8, W), row_off, jnp.int32)
    offs[j, 1] = jnp.full((8, W), col_off, jnp.int32)

    pl.semaphore_wait(barrier, NB - 1 + X - 1 + Z - 1 + 7)

    def strip(l, i):
        n = near[i]
        src, dst = (
            (obj.at[l, :, :, mine, 0:W], ext.at[l, :, 0:2, :, 2 * W :]),
            (obj.at[l, :, 0, mine, :], ext.at[l, :, 2, :, 0 : 2 * W]),
            (obj.at[l, :, 0, mine, 0:W], ext.at[l, :, 2, :, 2 * W :]),
        )[i]
        return pltpu.make_async_remote_copy(
            src, dst, f1_s.at[l, i], f1_r.at[l, i],
            device_id=(lax.rem(t + T - n, T), j), device_id_type=MESH,
        )

    def offs_copy(d):
        return pltpu.make_async_remote_copy(
            offs.at[j], offs.at[j], of_s.at[d - 1], of_r.at[d - 1],
            device_id=(t, y_dev(d)), device_id_type=MESH,
        )

    def offs_arrival(d):
        src = y_dev(NB - d)
        return pltpu.make_async_remote_copy(
            offs.at[src], offs.at[src], of_s.at[d - 1], of_r.at[d - 1],
            device_id=(t, src), device_id_type=MESH,
        )

    for i in range(3):
        strip(0, i).start()
    lax.fori_loop(1, NB, lambda d, c: (offs_copy(d).start(), c)[1], 0)
    for i in range(3):
        strip(1, i).start()

    for c in local[2:]:
        c.wait()
    ang = hph[0]
    hph[0] = jnp.cos(ang)
    hph[1] = jnp.sin(ang)
    r_in = jnp.bitwise_and(row_off, W - 1)
    c_in = jnp.bitwise_and(col_off, W - 1)
    for m in range(2):
        for q in range(2):
            v = prb[m, q * W : (q + 1) * W, :]
            prb[m, q * W : (q + 1) * W, :] = pltpu.roll(pltpu.roll(v, r_in, 0), c_in, 1)
    r_back = jnp.bitwise_and(W - r_in, W - 1)
    c_back = jnp.bitwise_and(W - c_in, W - 1)

    lanes = lax.broadcasted_iota(jnp.int32, (RC, W), 1)
    rows = lax.broadcasted_iota(jnp.int32, (RC, W), 0) + RC * cls(j)

    def masks(dev):
        ro = jnp.broadcast_to(offs[dev, 0, 0:1, :], (RC, W))
        co = jnp.broadcast_to(offs[dev, 1, 0:1, :], (RC, W))
        return (rows >= ro, rows >= ro - W), (lanes >= co, lanes >= co - W)

    def pick(m, a, b, c):
        return jnp.where(m[0], a, jnp.where(m[1], b, c))

    def selected(l, dev):
        rm, cm = masks(dev)
        out = []
        for q in range(2):
            part = [
                pick(cm, *(ext[l, q, b, :, k * W : (k + 1) * W] for k in range(3))) for b in range(3)
            ]
            out.append(pick(rm, *part))
        return out

    def f2_copy(l, d):
        return pltpu.make_async_remote_copy(
            sel.at[l, d - 1], win.at[l, :, mine, :], f2_s.at[l, d - 1], f2_r.at[l, d - 1],
            device_id=(t, y_dev(d)), device_id_type=MESH,
        )

    def f2_arrival(l, d):
        src = y_dev(NB - d)
        return pltpu.make_async_remote_copy(
            sel.at[l, d - 1], win.at[l, :, rows_of(src), :], f2_s.at[l, d - 1], f2_r.at[l, d - 1],
            device_id=(t, src), device_id_type=MESH,
        )

    def spread_window(l):
        def one(d, c):
            vals = selected(l, y_dev(d))
            for q in range(2):
                sel[l, d - 1, q] = vals[q]
            f2_copy(l, d).start()
            return c

        lax.fori_loop(1, NB, one, 0)
        vals = selected(l, j)
        for q in range(2):
            win[l, q, mine, :] = vals[q]

    for l in range(2):
        local[l].wait()
        for i in range(3):
            strip(l, i).wait_recv()
        if l == 0:
            lax.fori_loop(1, NB, lambda d, c: (offs_arrival(d).wait_recv(), c)[1], 0)
        spread_window(l)

    L, R = 0, 1

    def forward(d):
        return from_left(swap_blocks(from_right(d, trow[R])), tcol[L])

    def inverse(d):
        return from_right(swap_blocks(from_left(d, tcol[R])), trow[L])

    def forward_pr(d):
        return from_right(swap_blocks(from_left(d, tcol[L])), trow[R])

    def by_mode(blocks):
        return jnp.concatenate([jnp.concatenate(list(b), 1) for b in blocks], 0)

    def by_part(blocks):
        return jnp.concatenate(
            [jnp.concatenate([b[q] for b in blocks], 1) for q in range(2)], 0
        )

    def modes_of(d):
        return [(d[m * W : (m + 1) * W, :W], d[m * W : (m + 1) * W, W:]) for m in range(2)]

    def modes_of_pr(d):
        return [(d[:W, m * W : (m + 1) * W], d[W:, m * W : (m + 1) * W]) for m in range(2)]

    def mul(a, b):
        return a[0] * b[0] - a[1] * b[1], a[0] * b[1] + a[1] * b[0]

    def mul_conj(a, b):
        return a[0] * b[0] + a[1] * b[1], a[0] * b[1] - a[1] * b[0]

    def window(l):
        return win[l, 0], win[l, 1]

    def probe_mode(m):
        return prb[m, 0:W, :], prb[m, W:, :]

    def arrive_window(l):
        lax.fori_loop(1, NB, lambda d, c: (f2_arrival(l, d).wait_recv(), c)[1], 0)

    arrive_window(0)
    w0 = window(0)
    spec = forward(by_mode([mul(probe_mode(m), w0) for m in range(2)]))
    prop = (hph[0], hph[1])
    spec = by_part([mul(s, prop) for s in modes_of_pr(spec)])
    at1 = inverse(spec)
    mid[...] = at1
    arrive_window(1)
    w1 = window(1)
    far = forward(by_mode([mul(s, w1) for s in modes_of(at1)]))
    sq = far * far
    col = sq[:W, :] + sq[W:, :]
    err = (col[:, :W] + col[:, W:] - msr[...]) * (4.0 * LOSS_SCALE)
    err2 = jnp.concatenate([err, err], 1)
    back = inverse(far * jnp.concatenate([err2, err2], 0))
    gb = modes_of(back)
    ms = modes_of(mid[...])
    g1a, g1b = (mul_conj(ms[m], gb[m]) for m in range(2))
    gwin[1, 0] = g1a[0] + g1b[0]
    gwin[1, 1] = g1a[1] + g1b[1]

    def g1_copy(l, d):
        dev = y_dev(d)
        return pltpu.make_async_remote_copy(
            gwin.at[l, :, rows_of(dev), :], gbuf.at[j, l], g1_s.at[l, d - 1], g1_r.at[l, d - 1],
            device_id=(t, dev), device_id_type=MESH,
        )

    def g1_arrival(l, d):
        src = y_dev(NB - d)
        return pltpu.make_async_remote_copy(
            gwin.at[l, :, mine, :], gbuf.at[src, l], g1_s.at[l, d - 1], g1_r.at[l, d - 1],
            device_id=(t, src), device_id_type=MESH,
        )

    def spread_grad(l):
        lax.fori_loop(1, NB, lambda d, c: (g1_copy(l, d).start(), c)[1], 0)
        gbuf[j, l] = gwin[l, :, mine, :]

    spread_grad(1)
    w1 = window(1)
    spec = forward(by_mode([mul_conj(w1, g) for g in gb]))
    spec = by_part([mul_conj(prop, s) for s in modes_of_pr(spec)])
    gb = modes_of(inverse(spec))
    w0 = window(0)
    for m in range(2):
        gp = mul_conj(w0, gb[m])
        for q in range(2):
            pg[m, q * W : (q + 1) * W, :] = pltpu.roll(pltpu.roll(gp[q], c_back, 1), r_back, 0)
    core_copy = pltpu.make_async_remote_copy(
        pg.at[1 - core], p_core, pc_s, pc_r, device_id=(sib, j), device_id_type=MESH
    )
    core_copy.start()
    g0a, g0b = (mul_conj(probe_mode(m), gb[m]) for m in range(2))
    gwin[0, 0] = g0a[0] + g0b[0]
    gwin[0, 1] = g0a[1] + g0b[1]
    spread_grad(0)

    def px_rows(xx):
        return pl.ds(pl.multiple_of(XP * xx, XP), XP)

    def px_copy(d):
        xx = lax.rem(x + d, X)
        return pltpu.make_async_remote_copy(
            s_core.at[px_rows(xx)], p_x.at[d - 1], px_s.at[d - 1], px_r.at[d - 1],
            device_id=(x_tile(d), j), device_id_type=MESH,
        )

    def py_rows(yy):
        return pl.ds(pl.multiple_of(YP * yy, YP), YP)

    def py_copy(d):
        dev = y_dev(d)
        return pltpu.make_async_remote_copy(
            s_x.at[py_rows(dev)], p_y.at[d - 1], py_s.at[d - 1], py_r.at[d - 1],
            device_id=(t, dev), device_id_type=MESH,
        )

    def pz_copy(d):
        return pltpu.make_async_remote_copy(
            p_z.at[z], p_z.at[z], pz_s.at[d - 1], pz_r.at[d - 1],
            device_id=(z_tile(d), j), device_id_type=MESH,
        )

    def pz_arrival(d):
        zz = lax.rem(z + Z - d, Z)
        return pltpu.make_async_remote_copy(
            p_z.at[zz], p_z.at[zz], pz_s.at[d - 1], pz_r.at[d - 1],
            device_id=(z_tile(Z - d), j), device_id_type=MESH,
        )

    def out_rows(xx, yy):
        return pl.ds(pl.multiple_of(XP * xx + YP * yy, YP), YP)

    def qy_copy(d, arrival=False):
        own = y_dev(NB - d) if arrival else j
        piece = pout.at[core, out_rows(x, own)]
        return pltpu.make_async_remote_copy(
            piece, piece, qy_s.at[d - 1], qy_r.at[d - 1],
            device_id=(t, y_dev(d)), device_id_type=MESH,
        )

    def qx_copy(d, arrival=False):
        own = lax.rem(x + X - d, X) if arrival else x
        piece = pout.at[core, px_rows(own)]
        return pltpu.make_async_remote_copy(
            piece, piece, qx_s.at[d - 1], qx_r.at[d - 1],
            device_id=(x_tile(d), j), device_id_type=MESH,
        )

    def qc_copy(which):
        return pltpu.make_async_remote_copy(
            pout.at[which], pout.at[which], qc_s, qc_r, device_id=(sib, j), device_id_type=MESH
        )

    core_copy.wait_recv()
    s_core[...] = pg[core] + p_core[...]
    for d in range(1, X):
        px_copy(d).start()

    def gather_grad(l):
        lax.fori_loop(1, NB, lambda d, c: (g1_arrival(l, d).wait_recv(), c)[1], 0)
        acc[l] = jnp.zeros(acc.shape[1:], F32)

        def one(dev, c):
            rm, cm = masks(dev)
            rsel = (rm[0], rm[1] & ~rm[0], ~rm[1])
            csel = (cm[0], cm[1] & ~cm[0], ~cm[1])
            for q in range(2):
                g = gbuf[dev, l, q]
                for b in range(3):
                    gr = jnp.where(rsel[b], g, 0.0)
                    for k in range(3):
                        at = (l, q, b, slice(None), slice(k * W, (k + 1) * W))
                        acc[at] = acc[at] + jnp.where(csel[k], gr, 0.0)
            return c

        lax.fori_loop(0, NB, one, 0)
        for i in range(3):
            g2_copy(l, i).start()

    def g2_copy(l, i):
        n = near[i]
        src, dst = (
            (acc.at[l, :, 0:2, :, 2 * W :], r_right.at[l]),
            (acc.at[l, :, 2, :, 0 : 2 * W], r_low.at[l]),
            (acc.at[l, :, 2, :, 2 * W :], r_diag.at[l]),
        )[i]
        return pltpu.make_async_remote_copy(
            src, dst, g2_s.at[l, i], g2_r.at[l, i],
            device_id=(lax.rem(t + n, T), j), device_id_type=MESH,
        )

    side = j // half

    def g3_copy(l):
        return pltpu.make_async_remote_copy(
            fin.at[l, 1 - side], r_fin.at[l], g3_s.at[l], g3_r.at[l],
            device_id=(t, y_dev(half)), device_id_type=MESH,
        )

    def join_grad(l):
        for i in range(3):
            g2_copy(l, i).wait_recv()
        for q in range(2):
            for b in range(2):
                one = acc[l, q, b, :, 0:W] + r_right[l, q, b]
                two = acc[l, q, b, :, W : 2 * W]
                if b == 0:
                    one = one + r_low[l, q, :, 0:W] + r_diag[l, q]
                    two = two + r_low[l, q, :, W:]
                fin[l, b, q, :, 0:W] = one
                fin[l, b, q, :, W:] = two
        g3_copy(l).start()

    gather_grad(1)
    for d in range(1, X):
        px_copy(d).wait_recv()
    total = s_core[px_rows(x)]
    for d in range(1, X):
        total = total + p_x[d - 1]
    s_x[...] = total
    lax.fori_loop(1, NB, lambda d, c: (py_copy(d).start(), c)[1], 0)
    gather_grad(0)
    lax.fori_loop(1, NB, lambda d, c: (py_copy(d).wait_recv(), c)[1], 0)
    p_z[z] = lax.fori_loop(0, NB - 1, lambda i, v: v + p_y[i], s_x[py_rows(j)])
    lax.fori_loop(1, Z, lambda d, c: (pz_copy(d).start(), c)[1], 0)
    join_grad(1)
    join_grad(0)
    lax.fori_loop(1, Z, lambda d, c: (pz_arrival(d).wait_recv(), c)[1], 0)
    summed = lax.fori_loop(1, Z, lambda i, v: v + p_z[i], p_z[0])
    pout[core, out_rows(x, j)] = summed * (1.0 / (T * NB))
    lax.fori_loop(1, NB, lambda d, c: (qy_copy(d).start(), c)[1], 0)

    done = []
    for l in range(2):
        here = pltpu.make_async_copy(
            fin.at[l, side], out_g.at[l, :, pl.ds(pl.multiple_of(RC * side, RC), RC), :],
            loc_sem.at[7 + 2 * l],
        )
        here.start()
        g3_copy(l).wait_recv()
        there = pltpu.make_async_copy(
            r_fin.at[l], out_g.at[l, :, pl.ds(pl.multiple_of(RC * (1 - side), RC), RC), :],
            loc_sem.at[8 + 2 * l],
        )
        there.start()
        done += [here, there]

    lax.fori_loop(1, NB, lambda d, c: (qy_copy(d, True).wait_recv(), c)[1], 0)
    for d in range(1, X):
        qx_copy(d).start()
    for d in range(1, X):
        qx_copy(d, True).wait_recv()
    qc_copy(core).start()
    last = pltpu.make_async_copy(pout.at[core], out_p.at[core], loc_sem.at[11])
    last.start()
    qc_copy(1 - core).wait_recv()
    other = pltpu.make_async_copy(pout.at[1 - core], out_p.at[1 - core], loc_sem.at[12])
    other.start()
    done += [last, other]

    for l in range(2):
        for i in range(3):
            strip(l, i).wait_send()
            g2_copy(l, i).wait_send()
        g3_copy(l).wait_send()

    def sent_y(d, c):
        offs_copy(d).wait_send()
        for l in range(2):
            f2_copy(l, d).wait_send()
            g1_copy(l, d).wait_send()
        py_copy(d).wait_send()
        qy_copy(d).wait_send()
        return c

    lax.fori_loop(1, NB, sent_y, 0)
    lax.fori_loop(1, Z, lambda d, c: (pz_copy(d).wait_send(), c)[1], 0)
    for d in range(1, X):
        px_copy(d).wait_send()
        qx_copy(d).wait_send()
    core_copy.wait_send()
    qc_copy(core).wait_send()
    for c in done:
        c.wait()


def local(geo, trow, tcol, object_slices, probe, prop_phase, scan_offsets, measured):
    X, Z, NB, _ = geo
    RC = W // NB
    XP = 2 * W // X
    YP = XP // NB
    dma = pltpu.SemaphoreType.DMA
    vm = pltpu.VMEM
    any_spec = pl.BlockSpec(memory_space=pl.ANY)
    scratch = [
        vm((2, 2, 3, RC, 3 * W), F32),
        vm((2, 2, W, W), F32),
        vm((2, 2 * W, W), F32),
        vm((2, W, W), F32),
        vm((W, W), F32),
        vm((2, 6 * W, 2 * W), BF16),
        vm((2, 2 * W, 6 * W), BF16),
        vm((2 * W, 2 * W), F32),
        vm((NB, 2, 8, W), jnp.int32),
        vm((2, NB - 1, 2, RC, W), F32),
        vm((2, 2, W, W), F32),
        vm((NB, 2, 2, RC, W), F32),
        vm((2, 2, 3, RC, 3 * W), F32),
        vm((2, 2, 2, RC, W), F32),
        vm((2, 2, RC, 2 * W), F32),
        vm((2, 2, RC, W), F32),
        vm((2, 2, 2, RC, 2 * W), F32),
        vm((2, 2, RC, 2 * W), F32),
        vm((2, 2 * W, W), F32),
        vm((2 * W, W), F32),
        vm((2 * W, W), F32),
        vm((X - 1, XP, W), F32),
        vm((XP, W), F32),
        vm((NB - 1, YP, W), F32),
        vm((Z, YP, W), F32),
        vm((2, 2 * W, W), F32),
        dma((13,)),
        dma((2, 3)), dma((2, 3)), dma((NB - 1,)), dma((NB - 1,)),
        dma((2, NB - 1)), dma((2, NB - 1)), dma((2, NB - 1)), dma((2, NB - 1)),
        dma((2, 3)), dma((2, 3)), dma((2,)), dma((2,)),
        dma, dma, dma((X - 1,)), dma((X - 1,)), dma((NB - 1,)), dma((NB - 1,)),
        dma((max(Z - 1, 1),)), dma((max(Z - 1, 1),)), dma((NB - 1,)), dma((NB - 1,)),
        dma((X - 1,)), dma((X - 1,)), dma, dma,
    ]
    grad, step = pl.pallas_call(
        functools.partial(kernel, geo),
        out_shape=(
            jax.ShapeDtypeStruct((2, 2, 2 * RC, 2 * W), F32),
            jax.ShapeDtypeStruct((2, 2 * W, W), F32),
        ),
        in_specs=[pl.BlockSpec(memory_space=pltpu.SMEM)] + [any_spec] * 6,
        out_specs=(any_spec, any_spec),
        scratch_shapes=scratch,
        compiler_params=pltpu.CompilerParams(
            collective_id=0, has_side_effects=True, vmem_limit_bytes=48 * 1024 * 1024
        ),
        name="ptycho",
    )(
        scan_offsets.reshape(2),
        object_slices.reshape(2, 2, 2, W, 2 * W),
        probe.reshape(2, 2 * W, W),
        prop_phase,
        measured.reshape(W, W),
        trow,
        tcol,
    )
    return grad[None], step.reshape(2, 2, W, W)


def build(mesh, xs, tgx):
    nb = mesh.shape["batch"]
    geo = (xs, mesh.shape["tile"] // (2 * xs), nb, tgx)
    by_rows, by_cols = table_parts()
    in_specs = (
        P("tile", None, None, None, None),
        P(),
        P(),
        P("tile", "batch", None),
        P("tile", "batch", None, None),
    )
    out_specs = (P("tile", None, None, "batch", None), P())

    def run(*args):
        body = functools.partial(local, geo, jnp.asarray(by_rows), jnp.asarray(by_cols))
        return jax.shard_map(body, mesh=mesh, in_specs=in_specs, out_specs=out_specs, check_vma=False)(*args)

    return run


def solution(mesh):
    return build(mesh, XS, TGX)
```

```python
import functools
import math

import jax
import jax.numpy as jnp
import ml_dtypes
import numpy as np
from jax import lax
from jax.experimental import pallas as pl
from jax.experimental.pallas import tpu as pltpu
from jax.sharding import PartitionSpec as P

TGX = 8
XS = 4
LOSS_SCALE = 0.05
W = 128
F32 = jnp.float32
BF16 = jnp.bfloat16
MESH = pl.DeviceIdType.MESH


def table_parts():
    idx = np.arange(W)
    phase = (idx[:, None] * idx[None, :] % W) * (2.0 * math.pi / W)
    c, s = np.cos(phase) / math.sqrt(W), -np.sin(phase) / math.sqrt(W)
    left = np.block([[c, -s], [s, c]]).astype(np.float32)
    right = np.block([[c, s], [-s, c]]).astype(np.float32)

    def parts(m):
        hi = m.astype(ml_dtypes.bfloat16)
        return hi, (m - hi.astype(np.float32)).astype(ml_dtypes.bfloat16)

    lh, ll = parts(left)
    rh, rl = parts(right)
    by_rows = [np.concatenate([h, h, l], 0) for h, l in ((lh, ll), (rh, rl))]
    by_cols = [np.concatenate([h, l, h], 1) for h, l in ((lh, ll), (rh, rl))]
    return np.stack(by_rows), np.stack(by_cols)


def split(d):
    hi = d.astype(BF16)
    return hi, (d - hi.astype(F32)).astype(BF16)


def from_right(d, table):
    hi, lo = split(d)
    return jnp.dot(jnp.concatenate([hi, lo, hi], 1), table, preferred_element_type=F32)


def from_left(d, table):
    hi, lo = split(d)
    return jnp.dot(table, jnp.concatenate([hi, hi, lo], 0), preferred_element_type=F32)


def swap_blocks(d):
    top = jnp.concatenate([d[:W, :W], d[W:, :W]], 1)
    low = jnp.concatenate([d[:W, W:], d[W:, W:]], 1)
    return jnp.concatenate([top, low], 0)


def kernel(
    geo,
    offs_ref, obj, probe, phase, meas, trow_h, tcol_h,
    out_g, out_p,
    ext, win, prb, hph, msr, trow, tcol, mid, offs, sel,
    gwin, gbuf, acc, r_right, r_low, r_diag, fin, r_fin,
    pg, p_core, s_core, p_x, s_x, p_y, p_z, pout,
    loc_sem, f1_s, f1_r, of_s, of_r, f2_s, f2_r, g1_s, g1_r, g2_s, g2_r, g3_s, g3_r,
    pc_s, pc_r, px_s, px_r, py_s, py_r, pz_s, pz_r, qy_s, qy_r, qx_s, qx_r, qc_s, qc_r,
):
    X, Z, NB, tgx = geo
    T = X * Z * 2
    RC = W // NB
    XP = 2 * W // X
    YP = XP // NB
    half = NB // 2
    t = lax.axis_index("tile")
    j = lax.axis_index("batch")
    core = lax.rem(t, 2)
    z = lax.rem(t // 2, Z)
    x = t // (2 * Z)
    sib = t + 1 - 2 * core

    def z_tile(d):
        return (x * Z + lax.rem(z + d, Z)) * 2 + core

    def x_tile(d):
        return (lax.rem(x + d, X) * Z + z) * 2 + core

    def y_dev(d):
        return lax.rem(j + d, NB)

    def cls(dev):
        return 2 * lax.rem(dev, half) + dev // half

    def rows_of(dev):
        return pl.ds(pl.multiple_of(RC * cls(dev), RC), RC)

    near = (1, tgx, tgx + 1)

    barrier = pltpu.get_barrier_semaphore()

    def greet(tile, dev):
        pl.semaphore_signal(barrier, inc=1, device_id=(tile, dev), device_id_type=MESH)

    for n in near:
        greet(lax.rem(t + n, T), j)
        greet(lax.rem(t + T - n, T), j)
    greet(sib, j)
    lax.fori_loop(1, NB, lambda d, c: (greet(t, y_dev(d)), c)[1], 0)
    lax.fori_loop(1, X, lambda d, c: (greet(x_tile(d), j), c)[1], 0)
    lax.fori_loop(1, Z, lambda d, c: (greet(z_tile(d), j), c)[1], 0)

    mine = rows_of(j)
    local = [
        pltpu.make_async_copy(obj.at[l, :, :, mine, :], ext.at[l, :, 0:2, :, 0 : 2 * W], loc_sem.at[l])
        for l in range(2)
    ] + [
        pltpu.make_async_copy(a, b, loc_sem.at[2 + i])
        for i, (a, b) in enumerate(((probe, prb), (phase, hph.at[0]), (meas, msr), (trow_h, trow), (tcol_h, tcol)))
    ]
    for c in local:
        c.start()

    row_off = offs_ref[0]
    col_off = offs_ref[1]
    offs[j, 0] = jnp.full((8, W), row_off, jnp.int32)
    offs[j, 1] = jnp.full((8, W), col_off, jnp.int32)

    pl.semaphore_wait(barrier, NB - 1 + X - 1 + Z - 1 + 7)

    def strip(l, i):
        n = near[i]
        src, dst = (
            (obj.at[l, :, :, mine, 0:W], ext.at[l, :, 0:2, :, 2 * W :]),
            (obj.at[l, :, 0, mine, :], ext.at[l, :, 2, :, 0 : 2 * W]),
            (obj.at[l, :, 0, mine, 0:W], ext.at[l, :, 2, :, 2 * W :]),
        )[i]
        return pltpu.make_async_remote_copy(
            src, dst, f1_s.at[l, i], f1_r.at[l, i],
            device_id=(lax.rem(t + T - n, T), j), device_id_type=MESH,
        )

    def offs_copy(d):
        return pltpu.make_async_remote_copy(
            offs.at[j], offs.at[j], of_s.at[d - 1], of_r.at[d - 1],
            device_id=(t, y_dev(d)), device_id_type=MESH,
        )

    def offs_arrival(d):
        src = y_dev(NB - d)
        return pltpu.make_async_remote_copy(
            offs.at[src], offs.at[src], of_s.at[d - 1], of_r.at[d - 1],
            device_id=(t, src), device_id_type=MESH,
        )

    for i in range(3):
        strip(0, i).start()
    lax.fori_loop(1, NB, lambda d, c: (offs_copy(d).start(), c)[1], 0)
    for i in range(3):
        strip(1, i).start()

    for c in local[2:]:
        c.wait()
    ang = hph[0]
    hph[0] = jnp.cos(ang)
    hph[1] = jnp.sin(ang)
    r_in = jnp.bitwise_and(row_off, W - 1)
    c_in = jnp.bitwise_and(col_off, W - 1)
    for m in range(2):
        for q in range(2):
            v = prb[m, q * W : (q + 1) * W, :]
            prb[m, q * W : (q + 1) * W, :] = pltpu.roll(pltpu.roll(v, r_in, 0), c_in, 1)
    r_back = jnp.bitwise_and(W - r_in, W - 1)
    c_back = jnp.bitwise_and(W - c_in, W - 1)

    lanes = lax.broadcasted_iota(jnp.int32, (RC, W), 1)
    rows = lax.broadcasted_iota(jnp.int32, (RC, W), 0) + RC * cls(j)

    def masks(dev):
        ro = jnp.broadcast_to(offs[dev, 0, 0:1, :], (RC, W))
        co = jnp.broadcast_to(offs[dev, 1, 0:1, :], (RC, W))
        return (rows >= ro, rows >= ro - W), (lanes >= co, lanes >= co - W)

    def pick(m, a, b, c):
        return jnp.where(m[0], a, jnp.where(m[1], b, c))

    def selected(l, dev):
        rm, cm = masks(dev)
        out = []
        for q in range(2):
            part = [
                pick(cm, *(ext[l, q, b, :, k * W : (k + 1) * W] for k in range(3))) for b in range(3)
            ]
            out.append(pick(rm, *part))
        return out

    def f2_copy(l, d):
        return pltpu.make_async_remote_copy(
            sel.at[l, d - 1], win.at[l, :, mine, :], f2_s.at[l, d - 1], f2_r.at[l, d - 1],
            device_id=(t, y_dev(d)), device_id_type=MESH,
        )

    def f2_arrival(l, d):
        src = y_dev(NB - d)
        return pltpu.make_async_remote_copy(
            sel.at[l, d - 1], win.at[l, :, rows_of(src), :], f2_s.at[l, d - 1], f2_r.at[l, d - 1],
            device_id=(t, src), device_id_type=MESH,
        )

    def spread_window(l):
        def one(d, c):
            vals = selected(l, y_dev(d))
            for q in range(2):
                sel[l, d - 1, q] = vals[q]
            f2_copy(l, d).start()
            return c

        lax.fori_loop(1, NB, one, 0)
        vals = selected(l, j)
        for q in range(2):
            win[l, q, mine, :] = vals[q]

    for l in range(2):
        local[l].wait()
        for i in range(3):
            strip(l, i).wait_recv()
        if l == 0:
            lax.fori_loop(1, NB, lambda d, c: (offs_arrival(d).wait_recv(), c)[1], 0)
        spread_window(l)

    L, R = 0, 1

    def forward(d):
        return from_left(swap_blocks(from_right(d, trow[R])), tcol[L])

    def inverse(d):
        return from_right(swap_blocks(from_left(d, tcol[R])), trow[L])

    def forward_pr(d):
        return from_right(swap_blocks(from_left(d, tcol[L])), trow[R])

    def by_mode(blocks):
        return jnp.concatenate([jnp.concatenate(list(b), 1) for b in blocks], 0)

    def by_part(blocks):
        return jnp.concatenate(
            [jnp.concatenate([b[q] for b in blocks], 1) for q in range(2)], 0
        )

    def modes_of(d):
        return [(d[m * W : (m + 1) * W, :W], d[m * W : (m + 1) * W, W:]) for m in range(2)]

    def modes_of_pr(d):
        return [(d[:W, m * W : (m + 1) * W], d[W:, m * W : (m + 1) * W]) for m in range(2)]

    def mul(a, b):
        return a[0] * b[0] - a[1] * b[1], a[0] * b[1] + a[1] * b[0]

    def mul_conj(a, b):
        return a[0] * b[0] + a[1] * b[1], a[0] * b[1] - a[1] * b[0]

    def window(l):
        return win[l, 0], win[l, 1]

    def probe_mode(m):
        return prb[m, 0:W, :], prb[m, W:, :]

    def arrive_window(l):
        lax.fori_loop(1, NB, lambda d, c: (f2_arrival(l, d).wait_recv(), c)[1], 0)

    arrive_window(0)
    w0 = window(0)
    spec = forward(by_mode([mul(probe_mode(m), w0) for m in range(2)]))
    prop = (hph[0], hph[1])
    spec = by_part([mul(s, prop) for s in modes_of_pr(spec)])
    at1 = inverse(spec)
    mid[...] = at1
    arrive_window(1)
    w1 = window(1)
    far = forward(by_mode([mul(s, w1) for s in modes_of(at1)]))
    sq = far * far
    col = sq[:W, :] + sq[W:, :]
    err = (col[:, :W] + col[:, W:] - msr[...]) * (4.0 * LOSS_SCALE)
    err2 = jnp.concatenate([err, err], 1)
    back = inverse(far * jnp.concatenate([err2, err2], 0))
    gb = modes_of(back)
    ms = modes_of(mid[...])
    g1a, g1b = (mul_conj(ms[m], gb[m]) for m in range(2))
    gwin[1, 0] = g1a[0] + g1b[0]
    gwin[1, 1] = g1a[1] + g1b[1]

    def g1_copy(l, d):
        dev = y_dev(d)
        return pltpu.make_async_remote_copy(
            gwin.at[l, :, rows_of(dev), :], gbuf.at[j, l], g1_s.at[l, d - 1], g1_r.at[l, d - 1],
            device_id=(t, dev), device_id_type=MESH,
        )

    def g1_arrival(l, d):
        src = y_dev(NB - d)
        return pltpu.make_async_remote_copy(
            gwin.at[l, :, mine, :], gbuf.at[src, l], g1_s.at[l, d - 1], g1_r.at[l, d - 1],
            device_id=(t, src), device_id_type=MESH,
        )

    def spread_grad(l):
        lax.fori_loop(1, NB, lambda d, c: (g1_copy(l, d).start(), c)[1], 0)
        gbuf[j, l] = gwin[l, :, mine, :]

    spread_grad(1)
    w1 = window(1)
    spec = forward(by_mode([mul_conj(w1, g) for g in gb]))
    spec = by_part([mul_conj(prop, s) for s in modes_of_pr(spec)])
    gb = modes_of(inverse(spec))
    w0 = window(0)
    for m in range(2):
        gp = mul_conj(w0, gb[m])
        for q in range(2):
            pg[m, q * W : (q + 1) * W, :] = pltpu.roll(pltpu.roll(gp[q], c_back, 1), r_back, 0)
    core_copy = pltpu.make_async_remote_copy(
        pg.at[1 - core], p_core, pc_s, pc_r, device_id=(sib, j), device_id_type=MESH
    )
    core_copy.start()
    g0a, g0b = (mul_conj(probe_mode(m), gb[m]) for m in range(2))
    gwin[0, 0] = g0a[0] + g0b[0]
    gwin[0, 1] = g0a[1] + g0b[1]
    spread_grad(0)

    def px_rows(xx):
        return pl.ds(pl.multiple_of(XP * xx, XP), XP)

    def px_copy(d):
        xx = lax.rem(x + d, X)
        return pltpu.make_async_remote_copy(
            s_core.at[px_rows(xx)], p_x.at[d - 1], px_s.at[d - 1], px_r.at[d - 1],
            device_id=(x_tile(d), j), device_id_type=MESH,
        )

    def py_rows(yy):
        return pl.ds(pl.multiple_of(YP * yy, YP), YP)

    def py_copy(d):
        dev = y_dev(d)
        return pltpu.make_async_remote_copy(
            s_x.at[py_rows(dev)], p_y.at[d - 1], py_s.at[d - 1], py_r.at[d - 1],
            device_id=(t, dev), device_id_type=MESH,
        )

    def pz_copy(d):
        return pltpu.make_async_remote_copy(
            p_z.at[z], p_z.at[z], pz_s.at[d - 1], pz_r.at[d - 1],
            device_id=(z_tile(d), j), device_id_type=MESH,
        )

    def pz_arrival(d):
        zz = lax.rem(z + Z - d, Z)
        return pltpu.make_async_remote_copy(
            p_z.at[zz], p_z.at[zz], pz_s.at[d - 1], pz_r.at[d - 1],
            device_id=(z_tile(Z - d), j), device_id_type=MESH,
        )

    def out_rows(xx, yy):
        return pl.ds(pl.multiple_of(XP * xx + YP * yy, YP), YP)

    def qy_copy(d, arrival=False):
        own = y_dev(NB - d) if arrival else j
        piece = pout.at[core, out_rows(x, own)]
        return pltpu.make_async_remote_copy(
            piece, piece, qy_s.at[d - 1], qy_r.at[d - 1],
            device_id=(t, y_dev(d)), device_id_type=MESH,
        )

    def qx_copy(d, arrival=False):
        own = lax.rem(x + X - d, X) if arrival else x
        piece = pout.at[core, px_rows(own)]
        return pltpu.make_async_remote_copy(
            piece, piece, qx_s.at[d - 1], qx_r.at[d - 1],
            device_id=(x_tile(d), j), device_id_type=MESH,
        )

    def qc_copy(which):
        return pltpu.make_async_remote_copy(
            pout.at[which], pout.at[which], qc_s, qc_r, device_id=(sib, j), device_id_type=MESH
        )

    core_copy.wait_recv()
    s_core[...] = pg[core] + p_core[...]
    for d in range(1, X):
        px_copy(d).start()

    def gather_grad(l):
        lax.fori_loop(1, NB, lambda d, c: (g1_arrival(l, d).wait_recv(), c)[1], 0)
        acc[l] = jnp.zeros(acc.shape[1:], F32)

        def one(dev, c):
            rm, cm = masks(dev)
            rsel = (rm[0], rm[1] & ~rm[0], ~rm[1])
            csel = (cm[0], cm[1] & ~cm[0], ~cm[1])
            for q in range(2):
                g = gbuf[dev, l, q]
                for b in range(3):
                    gr = jnp.where(rsel[b], g, 0.0)
                    for k in range(3):
                        at = (l, q, b, slice(None), slice(k * W, (k + 1) * W))
                        acc[at] = acc[at] + jnp.where(csel[k], gr, 0.0)
            return c

        lax.fori_loop(0, NB, one, 0)
        for i in range(3):
            g2_copy(l, i).start()

    def g2_copy(l, i):
        n = near[i]
        src, dst = (
            (acc.at[l, :, 0:2, :, 2 * W :], r_right.at[l]),
            (acc.at[l, :, 2, :, 0 : 2 * W], r_low.at[l]),
            (acc.at[l, :, 2, :, 2 * W :], r_diag.at[l]),
        )[i]
        return pltpu.make_async_remote_copy(
            src, dst, g2_s.at[l, i], g2_r.at[l, i],
            device_id=(lax.rem(t + n, T), j), device_id_type=MESH,
        )

    side = j // half

    def g3_copy(l):
        return pltpu.make_async_remote_copy(
            fin.at[l, 1 - side], r_fin.at[l], g3_s.at[l], g3_r.at[l],
            device_id=(t, y_dev(half)), device_id_type=MESH,
        )

    def join_grad(l):
        for i in range(3):
            g2_copy(l, i).wait_recv()
        for q in range(2):
            for b in range(2):
                one = acc[l, q, b, :, 0:W] + r_right[l, q, b]
                two = acc[l, q, b, :, W : 2 * W]
                if b == 0:
                    one = one + r_low[l, q, :, 0:W] + r_diag[l, q]
                    two = two + r_low[l, q, :, W:]
                fin[l, b, q, :, 0:W] = one
                fin[l, b, q, :, W:] = two
        g3_copy(l).start()

    gather_grad(1)
    for d in range(1, X):
        px_copy(d).wait_recv()
    total = s_core[px_rows(x)]
    for d in range(1, X):
        total = total + p_x[d - 1]
    s_x[...] = total
    lax.fori_loop(1, NB, lambda d, c: (py_copy(d).start(), c)[1], 0)
    gather_grad(0)
    lax.fori_loop(1, NB, lambda d, c: (py_copy(d).wait_recv(), c)[1], 0)
    p_z[z] = lax.fori_loop(0, NB - 1, lambda i, v: v + p_y[i], s_x[py_rows(j)])
    lax.fori_loop(1, Z, lambda d, c: (pz_copy(d).start(), c)[1], 0)
    join_grad(1)
    join_grad(0)
    lax.fori_loop(1, Z, lambda d, c: (pz_arrival(d).wait_recv(), c)[1], 0)
    summed = lax.fori_loop(1, Z, lambda i, v: v + p_z[i], p_z[0])
    pout[core, out_rows(x, j)] = summed * (1.0 / (T * NB))
    lax.fori_loop(1, NB, lambda d, c: (qy_copy(d).start(), c)[1], 0)

    done = []
    for l in range(2):
        here = pltpu.make_async_copy(
            fin.at[l, side], out_g.at[l, :, pl.ds(pl.multiple_of(RC * side, RC), RC), :],
            loc_sem.at[7 + 2 * l],
        )
        here.start()
        g3_copy(l).wait_recv()
        there = pltpu.make_async_copy(
            r_fin.at[l], out_g.at[l, :, pl.ds(pl.multiple_of(RC * (1 - side), RC), RC), :],
            loc_sem.at[8 + 2 * l],
        )
        there.start()
        done += [here, there]

    lax.fori_loop(1, NB, lambda d, c: (qy_copy(d, True).wait_recv(), c)[1], 0)
    for d in range(1, X):
        qx_copy(d).start()
    for d in range(1, X):
        qx_copy(d, True).wait_recv()
    qc_copy(core).start()
    last = pltpu.make_async_copy(pout.at[core], out_p.at[core], loc_sem.at[11])
    last.start()
    qc_copy(1 - core).wait_recv()
    other = pltpu.make_async_copy(pout.at[1 - core], out_p.at[1 - core], loc_sem.at[12])
    other.start()
    done += [last, other]

    for l in range(2):
        for i in range(3):
            strip(l, i).wait_send()
            g2_copy(l, i).wait_send()
        g3_copy(l).wait_send()

    def sent_y(d, c):
        offs_copy(d).wait_send()
        for l in range(2):
            f2_copy(l, d).wait_send()
            g1_copy(l, d).wait_send()
        py_copy(d).wait_send()
        qy_copy(d).wait_send()
        return c

    lax.fori_loop(1, NB, sent_y, 0)
    lax.fori_loop(1, Z, lambda d, c: (pz_copy(d).wait_send(), c)[1], 0)
    for d in range(1, X):
        px_copy(d).wait_send()
        qx_copy(d).wait_send()
    core_copy.wait_send()
    qc_copy(core).wait_send()
    for c in done:
        c.wait()


def local(geo, trow, tcol, object_slices, probe, prop_phase, scan_offsets, measured):
    X, Z, NB, _ = geo
    RC = W // NB
    XP = 2 * W // X
    YP = XP // NB
    dma = pltpu.SemaphoreType.DMA
    vm = pltpu.VMEM
    any_spec = pl.BlockSpec(memory_space=pltpu.HBM)
    scratch = [
        vm((2, 2, 3, RC, 3 * W), F32),
        vm((2, 2, W, W), F32),
        vm((2, 2 * W, W), F32),
        vm((2, W, W), F32),
        vm((W, W), F32),
        vm((2, 6 * W, 2 * W), BF16),
        vm((2, 2 * W, 6 * W), BF16),
        vm((2 * W, 2 * W), F32),
        vm((NB, 2, 8, W), jnp.int32),
        vm((2, NB - 1, 2, RC, W), F32),
        vm((2, 2, W, W), F32),
        vm((NB, 2, 2, RC, W), F32),
        vm((2, 2, 3, RC, 3 * W), F32),
        vm((2, 2, 2, RC, W), F32),
        vm((2, 2, RC, 2 * W), F32),
        vm((2, 2, RC, W), F32),
        vm((2, 2, 2, RC, 2 * W), F32),
        vm((2, 2, RC, 2 * W), F32),
        vm((2, 2 * W, W), F32),
        vm((2 * W, W), F32),
        vm((2 * W, W), F32),
        vm((X - 1, XP, W), F32),
        vm((XP, W), F32),
        vm((NB - 1, YP, W), F32),
        vm((Z, YP, W), F32),
        vm((2, 2 * W, W), F32),
        dma((13,)),
        dma((2, 3)), dma((2, 3)), dma((NB - 1,)), dma((NB - 1,)),
        dma((2, NB - 1)), dma((2, NB - 1)), dma((2, NB - 1)), dma((2, NB - 1)),
        dma((2, 3)), dma((2, 3)), dma((2,)), dma((2,)),
        dma, dma, dma((X - 1,)), dma((X - 1,)), dma((NB - 1,)), dma((NB - 1,)),
        dma((max(Z - 1, 1),)), dma((max(Z - 1, 1),)), dma((NB - 1,)), dma((NB - 1,)),
        dma((X - 1,)), dma((X - 1,)), dma, dma,
    ]
    grad, step = pl.pallas_call(
        functools.partial(kernel, geo),
        out_shape=(
            jax.ShapeDtypeStruct((2, 2, 2 * RC, 2 * W), F32),
            jax.ShapeDtypeStruct((2, 2 * W, W), F32),
        ),
        in_specs=[pl.BlockSpec(memory_space=pltpu.SMEM)] + [any_spec] * 6,
        out_specs=(any_spec, any_spec),
        scratch_shapes=scratch,
        compiler_params=pltpu.CompilerParams(
            collective_id=0, has_side_effects=True, vmem_limit_bytes=48 * 1024 * 1024
        ),
        name="ptycho",
    )(
        *(
            pltpu.with_memory_space_constraint(a, pltpu.HBM)
            for a in (
                scan_offsets.reshape(2),
                object_slices.reshape(2, 2, 2, W, 2 * W),
                probe.reshape(2, 2 * W, W),
                prop_phase,
                measured.reshape(W, W),
                trow,
                tcol,
            )
        ),
    )
    return grad[None], step.reshape(2, 2, W, W)


def build(mesh, xs, tgx):
    nb = mesh.shape["batch"]
    geo = (xs, mesh.shape["tile"] // (2 * xs), nb, tgx)
    by_rows, by_cols = table_parts()
    in_specs = (
        P("tile", None, None, None, None),
        P(),
        P(),
        P("tile", "batch", None),
        P("tile", "batch", None, None),
    )
    out_specs = (P("tile", None, None, "batch", None), P())

    def run(*args):
        body = functools.partial(local, geo, jnp.asarray(by_rows), jnp.asarray(by_cols))
        return jax.shard_map(body, mesh=mesh, in_specs=in_specs, out_specs=out_specs, check_vma=False)(*args)

    return run


def solution(mesh):
    return build(mesh, XS, TGX)
```

```python
import functools
import math

import jax
import jax.numpy as jnp
import ml_dtypes
import numpy as np
from jax import lax
from jax.experimental import pallas as pl
from jax.experimental.pallas import tpu as pltpu
from jax.sharding import PartitionSpec as P

TGX = 8
XS = 4
LOSS_SCALE = 0.05
W = 128
F32 = jnp.float32
BF16 = jnp.bfloat16
MESH = pl.DeviceIdType.MESH


def table_parts():
    idx = np.arange(W)
    phase = (idx[:, None] * idx[None, :] % W) * (2.0 * math.pi / W)
    c, s = np.cos(phase) / math.sqrt(W), -np.sin(phase) / math.sqrt(W)
    left = np.block([[c, -s], [s, c]]).astype(np.float32)
    right = np.block([[c, s], [-s, c]]).astype(np.float32)

    def parts(m):
        hi = m.astype(ml_dtypes.bfloat16)
        return hi, (m - hi.astype(np.float32)).astype(ml_dtypes.bfloat16)

    lh, ll = parts(left)
    rh, rl = parts(right)
    by_rows = [np.concatenate([h, h, l], 0) for h, l in ((lh, ll), (rh, rl))]
    by_cols = [np.concatenate([h, l, h], 1) for h, l in ((lh, ll), (rh, rl))]
    return np.stack(by_rows), np.stack(by_cols)


def split(d):
    hi = d.astype(BF16)
    return hi, (d - hi.astype(F32)).astype(BF16)


def from_right(d, table):
    hi, lo = split(d)
    return jnp.dot(jnp.concatenate([hi, lo, hi], 1), table, preferred_element_type=F32)


def from_left(d, table):
    hi, lo = split(d)
    return jnp.dot(table, jnp.concatenate([hi, hi, lo], 0), preferred_element_type=F32)


def swap_blocks(d):
    top = jnp.concatenate([d[:W, :W], d[W:, :W]], 1)
    low = jnp.concatenate([d[:W, W:], d[W:, W:]], 1)
    return jnp.concatenate([top, low], 0)


def kernel(
    geo,
    offs_ref, obj, probe, phase, meas, trow_h, tcol_h,
    out_g, out_p,
    ext, win, prb, hph, msr, trow, tcol, mid, offs, sel,
    gwin, gbuf, acc, low, r_right, r_low, fin,
    pg, p_core, s_core, p_x, s_x, p_y, p_z, tile,
    loc_sem, f1_s, f1_r, of_s, of_r, f2_s, f2_r, g1_s, g1_r, g2_s, g2_r, g3_s, g3_r,
    pc_s, pc_r, px_s, px_r, py_s, py_r, pz_s, pz_r, qy_s, qy_r, qx_s, qx_r, qc_s, qc_r, beyond,
):
    X, Z, NB, tgx = geo
    T = X * Z * 2
    RC = W // NB
    XP = 2 * W // X
    YP = XP // NB
    half = NB // 2
    t = lax.axis_index("tile")
    j = lax.axis_index("batch")
    core = lax.rem(t, 2)
    z = lax.rem(t // 2, Z)
    x = t // (2 * Z)
    sib = t + 1 - 2 * core

    def z_tile(d):
        return (x * Z + lax.rem(z + d, Z)) * 2 + core

    def x_tile(d):
        return (lax.rem(x + d, X) * Z + z) * 2 + core

    def y_dev(d):
        return lax.rem(j + d, NB)

    def cls(dev):
        return 2 * lax.rem(dev, half) + dev // half

    def rows_of(dev):
        return pl.ds(pl.multiple_of(RC * cls(dev), RC), RC)

    near = (1, tgx, 1)
    reach = 4 if Z > 9 else Z - 1

    barrier = pltpu.get_barrier_semaphore()

    def greet(tile, dev):
        pl.semaphore_signal(barrier, inc=1, device_id=(tile, dev), device_id_type=MESH)

    for n in near[:2]:
        greet(lax.rem(t + n, T), j)
        greet(lax.rem(t + T - n, T), j)
    greet(sib, j)
    lax.fori_loop(1, NB, lambda d, c: (greet(t, y_dev(d)), c)[1], 0)
    lax.fori_loop(1, X, lambda d, c: (greet(x_tile(d), j), c)[1], 0)
    lax.fori_loop(1, reach + 1, lambda d, c: (greet(z_tile(d), j), c)[1], 0)
    more = reach if Z > 9 else 0
    lax.fori_loop(Z - more, Z, lambda d, c: (greet(z_tile(d), j), c)[1], 0)

    mine = rows_of(j)
    local = [
        pltpu.make_async_copy(obj.at[l, :, :, mine, :], ext.at[l, :, 0:2, :, 0 : 2 * W], loc_sem.at[l])
        for l in range(2)
    ] + [
        pltpu.make_async_copy(a, b, loc_sem.at[2 + i])
        for i, (a, b) in enumerate(((probe, prb), (phase, hph.at[0]), (meas, msr), (trow_h, trow), (tcol_h, tcol)))
    ]
    for c in local:
        c.start()

    row_off = offs_ref[0]
    col_off = offs_ref[1]
    offs[j, 0] = jnp.full((8, W), row_off, jnp.int32)
    offs[j, 1] = jnp.full((8, W), col_off, jnp.int32)

    pl.semaphore_wait(barrier, NB - 1 + X - 1 + reach + more + 5)
    for d in (reach, Z - reach) if more else ():
        pl.semaphore_signal(beyond, inc=1, device_id=(z_tile(d), j), device_id_type=MESH)

    def strip(l, i):
        n = near[i]
        src, dst = (
            (obj.at[l, :, :, mine, 0:W], ext.at[l, :, 0:2, :, 2 * W :]),
            (obj.at[l, :, 0, mine, :], ext.at[l, :, 2, :, 0 : 2 * W]),
            (ext.at[l, :, 2, :, 0:W], ext.at[l, :, 2, :, 2 * W :]),
        )[i]
        return pltpu.make_async_remote_copy(
            src, dst, f1_s.at[l, i], f1_r.at[l, i],
            device_id=(lax.rem(t + T - n, T), j), device_id_type=MESH,
        )

    def offs_copy(d):
        return pltpu.make_async_remote_copy(
            offs.at[j], offs.at[j], of_s.at[d - 1], of_r.at[d - 1],
            device_id=(t, y_dev(d)), device_id_type=MESH,
        )

    def offs_arrival(d):
        src = y_dev(NB - d)
        return pltpu.make_async_remote_copy(
            offs.at[src], offs.at[src], of_s.at[d - 1], of_r.at[d - 1],
            device_id=(t, src), device_id_type=MESH,
        )

    for i in (1, 0):
        strip(0, i).start()
    lax.fori_loop(1, NB, lambda d, c: (offs_copy(d).start(), c)[1], 0)
    for i in (1, 0):
        strip(1, i).start()

    for c in local[2:]:
        c.wait()
    ang = hph[0]
    hph[0] = jnp.cos(ang)
    hph[1] = jnp.sin(ang)
    r_in = jnp.bitwise_and(row_off, W - 1)
    c_in = jnp.bitwise_and(col_off, W - 1)
    for m in range(2):
        for q in range(2):
            v = prb[m, q * W : (q + 1) * W, :]
            prb[m, q * W : (q + 1) * W, :] = pltpu.roll(pltpu.roll(v, r_in, 0), c_in, 1)
    r_back = jnp.bitwise_and(W - r_in, W - 1)
    c_back = jnp.bitwise_and(W - c_in, W - 1)

    lanes = lax.broadcasted_iota(jnp.int32, (RC, W), 1)
    rows = lax.broadcasted_iota(jnp.int32, (RC, W), 0) + RC * cls(j)

    def masks(dev):
        ro = jnp.broadcast_to(offs[dev, 0, 0:1, :], (RC, W))
        co = jnp.broadcast_to(offs[dev, 1, 0:1, :], (RC, W))
        return (rows >= ro, rows >= ro - W), (lanes >= co, lanes >= co - W)

    def pick(m, a, b, c):
        return jnp.where(m[0], a, jnp.where(m[1], b, c))

    def selected(l, dev):
        rm, cm = masks(dev)
        out = []
        for q in range(2):
            part = [
                pick(cm, *(ext[l, q, b, :, k * W : (k + 1) * W] for k in range(3))) for b in range(3)
            ]
            out.append(pick(rm, *part))
        return out

    def f2_copy(l, d):
        return pltpu.make_async_remote_copy(
            sel.at[l, d - 1], win.at[l, :, mine, :], f2_s.at[l, d - 1], f2_r.at[l, d - 1],
            device_id=(t, y_dev(d)), device_id_type=MESH,
        )

    def f2_arrival(l, d):
        src = y_dev(NB - d)
        return pltpu.make_async_remote_copy(
            sel.at[l, d - 1], win.at[l, :, rows_of(src), :], f2_s.at[l, d - 1], f2_r.at[l, d - 1],
            device_id=(t, src), device_id_type=MESH,
        )

    def spread_window(l):
        def one(d, c):
            vals = selected(l, y_dev(d))
            for q in range(2):
                sel[l, d - 1, q] = vals[q]
            f2_copy(l, d).start()
            return c

        lax.fori_loop(1, NB, one, 0)
        vals = selected(l, j)
        for q in range(2):
            win[l, q, mine, :] = vals[q]

    for l in range(2):
        local[l].wait()
        strip(l, 1).wait_recv()
        strip(l, 2).start()
        for i in (0, 2):
            strip(l, i).wait_recv()
        if l == 0:
            lax.fori_loop(1, NB, lambda d, c: (offs_arrival(d).wait_recv(), c)[1], 0)
        spread_window(l)

    L, R = 0, 1

    def forward(d):
        return from_left(swap_blocks(from_right(d, trow[R])), tcol[L])

    def inverse(d):
        return from_right(swap_blocks(from_left(d, tcol[R])), trow[L])

    def forward_pr(d):
        return from_right(swap_blocks(from_left(d, tcol[L])), trow[R])

    def by_mode(blocks):
        return jnp.concatenate([jnp.concatenate(list(b), 1) for b in blocks], 0)

    def by_part(blocks):
        return jnp.concatenate(
            [jnp.concatenate([b[q] for b in blocks], 1) for q in range(2)], 0
        )

    def modes_of(d):
        return [(d[m * W : (m + 1) * W, :W], d[m * W : (m + 1) * W, W:]) for m in range(2)]

    def modes_of_pr(d):
        return [(d[:W, m * W : (m + 1) * W], d[W:, m * W : (m + 1) * W]) for m in range(2)]

    def mul(a, b):
        return a[0] * b[0] - a[1] * b[1], a[0] * b[1] + a[1] * b[0]

    def mul_conj(a, b):
        return a[0] * b[0] + a[1] * b[1], a[0] * b[1] - a[1] * b[0]

    def window(l):
        return win[l, 0], win[l, 1]

    def probe_mode(m):
        return prb[m, 0:W, :], prb[m, W:, :]

    def arrive_window(l):
        lax.fori_loop(1, NB, lambda d, c: (f2_arrival(l, d).wait_recv(), c)[1], 0)

    arrive_window(0)
    w0 = window(0)
    spec = forward(by_mode([mul(probe_mode(m), w0) for m in range(2)]))
    prop = (hph[0], hph[1])
    spec = by_part([mul(s, prop) for s in modes_of_pr(spec)])
    at1 = inverse(spec)
    mid[...] = at1
    arrive_window(1)
    w1 = window(1)
    far = forward(by_mode([mul(s, w1) for s in modes_of(at1)]))
    sq = far * far
    col = sq[:W, :] + sq[W:, :]
    err = (col[:, :W] + col[:, W:] - msr[...]) * (4.0 * LOSS_SCALE)
    err2 = jnp.concatenate([err, err], 1)
    back = inverse(far * jnp.concatenate([err2, err2], 0))
    gb = modes_of(back)
    ms = modes_of(mid[...])
    g1a, g1b = (mul_conj(ms[m], gb[m]) for m in range(2))
    gwin[1, 0] = g1a[0] + g1b[0]
    gwin[1, 1] = g1a[1] + g1b[1]

    def g1_copy(l, d):
        dev = y_dev(d)
        return pltpu.make_async_remote_copy(
            gwin.at[l, :, rows_of(dev), :], gbuf.at[j, l], g1_s.at[l, d - 1], g1_r.at[l, d - 1],
            device_id=(t, dev), device_id_type=MESH,
        )

    def g1_arrival(l, d):
        src = y_dev(NB - d)
        return pltpu.make_async_remote_copy(
            gwin.at[l, :, mine, :], gbuf.at[src, l], g1_s.at[l, d - 1], g1_r.at[l, d - 1],
            device_id=(t, src), device_id_type=MESH,
        )

    def spread_grad(l):
        lax.fori_loop(1, NB, lambda d, c: (g1_copy(l, d).start(), c)[1], 0)
        gbuf[j, l] = gwin[l, :, mine, :]

    spread_grad(1)
    w1 = window(1)
    spec = forward(by_mode([mul_conj(w1, g) for g in gb]))
    spec = by_part([mul_conj(prop, s) for s in modes_of_pr(spec)])
    gb = modes_of(inverse(spec))
    w0 = window(0)
    for m in range(2):
        gp = mul_conj(w0, gb[m])
        for q in range(2):
            pg[m, q * W : (q + 1) * W, :] = pltpu.roll(pltpu.roll(gp[q], c_back, 1), r_back, 0)
    core_copy = pltpu.make_async_remote_copy(
        pg.at[1 - core], p_core, pc_s, pc_r, device_id=(sib, j), device_id_type=MESH
    )
    core_copy.start()
    g0a, g0b = (mul_conj(probe_mode(m), gb[m]) for m in range(2))
    gwin[0, 0] = g0a[0] + g0b[0]
    gwin[0, 1] = g0a[1] + g0b[1]
    spread_grad(0)

    def px_rows(xx):
        return pl.ds(pl.multiple_of(XP * xx, XP), XP)

    def px_copy(d):
        xx = lax.rem(x + d, X)
        return pltpu.make_async_remote_copy(
            s_core.at[px_rows(xx)], p_x.at[d - 1], px_s.at[d - 1], px_r.at[d - 1],
            device_id=(x_tile(d), j), device_id_type=MESH,
        )

    def py_rows(yy):
        return pl.ds(pl.multiple_of(YP * yy, YP), YP)

    def py_copy(d):
        dev = y_dev(d)
        return pltpu.make_async_remote_copy(
            s_x.at[py_rows(dev)], p_y.at[d - 1], py_s.at[d - 1], py_r.at[d - 1],
            device_id=(t, dev), device_id_type=MESH,
        )

    def pz_copy(d):
        return pltpu.make_async_remote_copy(
            p_z.at[z], p_z.at[z], pz_s.at[d - 1], pz_r.at[d - 1],
            device_id=(z_tile(d), j), device_id_type=MESH,
        )

    def pz_arrival(d):
        zz = lax.rem(z + Z - d, Z)
        return pltpu.make_async_remote_copy(
            p_z.at[zz], p_z.at[zz], pz_s.at[d - 1], pz_r.at[d - 1],
            device_id=(z_tile(Z - d), j), device_id_type=MESH,
        )

    def out_rows(xx, yy):
        return pl.ds(pl.multiple_of(XP * xx + YP * yy, YP), YP)

    def qy_copy(d, arrival=False):
        own = y_dev(NB - d) if arrival else j
        return pltpu.make_async_remote_copy(
            tile, out_p.at[core, out_rows(x, own)], qy_s.at[d - 1], qy_r.at[d - 1],
            device_id=(t, y_dev(d)), device_id_type=MESH,
        )

    def qx_copy(d, arrival=False):
        own = lax.rem(x + X - d, X) if arrival else x
        piece = out_p.at[core, px_rows(own)]
        return pltpu.make_async_remote_copy(
            piece, piece, qx_s.at[d - 1], qx_r.at[d - 1],
            device_id=(x_tile(d), j), device_id_type=MESH,
        )

    def qc_copy(d, which):
        piece = out_p.at[which, px_rows(lax.rem(x + X - d, X))]
        return pltpu.make_async_remote_copy(
            piece, piece, qc_s.at[d], qc_r.at[d], device_id=(sib, j), device_id_type=MESH
        )

    core_copy.wait_recv()
    s_core[...] = pg[core] + p_core[...]
    for d in range(1, X):
        px_copy(d).start()

    def gather_grad(l):
        lax.fori_loop(1, NB, lambda d, c: (g1_arrival(l, d).wait_recv(), c)[1], 0)
        acc[l] = jnp.zeros(acc.shape[1:], F32)

        def one(dev, c):
            rm, cm = masks(dev)
            rsel = (rm[0], rm[1] & ~rm[0], ~rm[1])
            csel = (cm[0], cm[1] & ~cm[0], ~cm[1])
            for q in range(2):
                g = gbuf[dev, l, q]
                for b in range(3):
                    gr = jnp.where(rsel[b], g, 0.0)
                    for k in range(3):
                        at = (l, q, b, slice(None), slice(k * W, (k + 1) * W))
                        acc[at] = acc[at] + jnp.where(csel[k], gr, 0.0)
            return c

        lax.fori_loop(0, NB, one, 0)
        g2_copy(l, 0).start()

    def g2_copy(l, i):
        src, dst = ((acc.at[l, :, :, :, 2 * W :], r_right.at[l]), (low.at[l], r_low.at[l]))[i]
        return pltpu.make_async_remote_copy(
            src, dst, g2_s.at[l, i], g2_r.at[l, i],
            device_id=(lax.rem(t + near[i], T), j), device_id_type=MESH,
        )

    def pass_low(l):
        g2_copy(l, 0).wait_recv()
        for q in range(2):
            low[l, q, :, 0:W] = acc[l, q, 2, :, 0:W] + r_right[l, q, 2]
            low[l, q, :, W:] = acc[l, q, 2, :, W : 2 * W]
        g2_copy(l, 1).start()

    side = j // half

    def g_rows(which):
        return pl.ds(pl.multiple_of(RC * which, RC), RC)

    def g3_copy(l, which):
        return pltpu.make_async_remote_copy(
            fin.at[l, 1 - side], out_g.at[l, :, g_rows(which), :], g3_s.at[l], g3_r.at[l],
            device_id=(t, y_dev(half)), device_id_type=MESH,
        )

    def g_here(l):
        return pltpu.make_async_copy(fin.at[l, side], out_g.at[l, :, g_rows(side), :], loc_sem.at[7 + l])

    def join_grad(l):
        g2_copy(l, 1).wait_recv()
        for q in range(2):
            for b in range(2):
                one = acc[l, q, b, :, 0:W] + r_right[l, q, b]
                two = acc[l, q, b, :, W : 2 * W]
                if b == 0:
                    one = one + r_low[l, q, :, 0:W]
                    two = two + r_low[l, q, :, W:]
                fin[l, b, q, :, 0:W] = one
                fin[l, b, q, :, W:] = two
        g3_copy(l, side).start()
        g_here(l).start()

    gather_grad(1)
    for d in range(1, X):
        px_copy(d).wait_recv()
    total = s_core[px_rows(x)]
    for d in range(1, X):
        total = total + p_x[d - 1]
    s_x[...] = total
    lax.fori_loop(1, NB, lambda d, c: (py_copy(d).start(), c)[1], 0)
    gather_grad(0)
    pass_low(1)
    lax.fori_loop(1, NB, lambda d, c: (py_copy(d).wait_recv(), c)[1], 0)
    p_z[z] = lax.fori_loop(0, NB - 1, lambda i, v: v + p_y[i], s_x[py_rows(j)])
    if more:
        pl.semaphore_wait(beyond, 2)
    lax.fori_loop(1, Z, lambda d, c: (pz_copy(d).start(), c)[1], 0)
    pass_low(0)
    join_grad(1)
    lax.fori_loop(1, Z, lambda d, c: (pz_arrival(d).wait_recv(), c)[1], 0)
    summed = lax.fori_loop(1, Z, lambda i, v: v + p_z[i], p_z[0])
    tile[...] = summed * (1.0 / (T * NB))
    lax.fori_loop(1, NB, lambda d, c: (qy_copy(d).start(), c)[1], 0)
    keep = pltpu.make_async_copy(tile, out_p.at[core, out_rows(x, j)], loc_sem.at[9])
    keep.start()
    join_grad(0)
    keep.wait()
    lax.fori_loop(1, NB, lambda d, c: (qy_copy(d, True).wait_recv(), c)[1], 0)
    for d in range(1, X):
        qx_copy(d).start()
    qc_copy(0, core).start()
    for d in range(1, X):
        qx_copy(d, True).wait_recv()
        qc_copy(d, core).start()

    for l in range(2):
        for i in range(3):
            strip(l, i).wait_send()
        for i in range(2):
            g2_copy(l, i).wait_send()
        g3_copy(l, side).wait_send()

    def sent_y(d, c):
        offs_copy(d).wait_send()
        for l in range(2):
            f2_copy(l, d).wait_send()
            g1_copy(l, d).wait_send()
        py_copy(d).wait_send()
        qy_copy(d).wait_send()
        return c

    lax.fori_loop(1, NB, sent_y, 0)
    lax.fori_loop(1, Z, lambda d, c: (pz_copy(d).wait_send(), c)[1], 0)
    for d in range(1, X):
        px_copy(d).wait_send()
        qx_copy(d).wait_send()
    core_copy.wait_send()
    for l in range(2):
        g_here(l).wait()
        g3_copy(l, 1 - side).wait_recv()
    for d in range(X):
        qc_copy(d, core).wait_send()
    for d in range(X):
        qc_copy(d, 1 - core).wait_recv()


def local(geo, trow, tcol, object_slices, probe, prop_phase, scan_offsets, measured):
    X, Z, NB, _ = geo
    RC = W // NB
    XP = 2 * W // X
    YP = XP // NB
    dma = pltpu.SemaphoreType.DMA
    vm = pltpu.VMEM
    any_spec = pl.BlockSpec(memory_space=pltpu.HBM)
    scratch = [
        vm((2, 2, 3, RC, 3 * W), F32),
        vm((2, 2, W, W), F32),
        vm((2, 2 * W, W), F32),
        vm((2, W, W), F32),
        vm((W, W), F32),
        vm((2, 6 * W, 2 * W), BF16),
        vm((2, 2 * W, 6 * W), BF16),
        vm((2 * W, 2 * W), F32),
        vm((NB, 2, 8, W), jnp.int32),
        vm((2, NB - 1, 2, RC, W), F32),
        vm((2, 2, W, W), F32),
        vm((NB, 2, 2, RC, W), F32),
        vm((2, 2, 3, RC, 3 * W), F32),
        vm((2, 2, RC, 2 * W), F32),
        vm((2, 2, 3, RC, W), F32),
        vm((2, 2, RC, 2 * W), F32),
        vm((2, 2, 2, RC, 2 * W), F32),
        vm((2, 2 * W, W), F32),
        vm((2 * W, W), F32),
        vm((2 * W, W), F32),
        vm((X - 1, XP, W), F32),
        vm((XP, W), F32),
        vm((NB - 1, YP, W), F32),
        vm((Z, YP, W), F32),
        vm((YP, W), F32),
        dma((10,)),
        dma((2, 3)), dma((2, 3)), dma((NB - 1,)), dma((NB - 1,)),
        dma((2, NB - 1)), dma((2, NB - 1)), dma((2, NB - 1)), dma((2, NB - 1)),
        dma((2, 2)), dma((2, 2)), dma((2,)), dma((2,)),
        dma, dma, dma((X - 1,)), dma((X - 1,)), dma((NB - 1,)), dma((NB - 1,)),
        dma((max(Z - 1, 1),)), dma((max(Z - 1, 1),)), dma((NB - 1,)), dma((NB - 1,)),
        dma((X - 1,)), dma((X - 1,)), dma((X,)), dma((X,)), pltpu.SemaphoreType.REGULAR,
    ]
    grad, step = pl.pallas_call(
        functools.partial(kernel, geo),
        out_shape=(
            jax.ShapeDtypeStruct((2, 2, 2 * RC, 2 * W), F32),
            jax.ShapeDtypeStruct((2, 2 * W, W), F32),
        ),
        in_specs=[pl.BlockSpec(memory_space=pltpu.SMEM)] + [any_spec] * 6,
        out_specs=(any_spec, any_spec),
        scratch_shapes=scratch,
        compiler_params=pltpu.CompilerParams(
            collective_id=0, has_side_effects=True, vmem_limit_bytes=48 * 1024 * 1024
        ),
        name="ptycho",
    )(
        *(
            pltpu.with_memory_space_constraint(a, pltpu.HBM)
            for a in (
                scan_offsets.reshape(2),
                object_slices.reshape(2, 2, 2, W, 2 * W),
                probe.reshape(2, 2 * W, W),
                prop_phase,
                measured.reshape(W, W),
                trow,
                tcol,
            )
        ),
    )
    return grad[None], step.reshape(2, 2, W, W)


def build(mesh, xs, tgx):
    nb = mesh.shape["batch"]
    geo = (xs, mesh.shape["tile"] // (2 * xs), nb, tgx)
    by_rows, by_cols = table_parts()
    in_specs = (
        P("tile", None, None, None, None),
        P(),
        P(),
        P("tile", "batch", None),
        P("tile", "batch", None, None),
    )
    out_specs = (P("tile", None, None, "batch", None), P())

    def run(*args):
        body = functools.partial(local, geo, jnp.asarray(by_rows), jnp.asarray(by_cols))
        return jax.shard_map(body, mesh=mesh, in_specs=in_specs, out_specs=out_specs, check_vma=False)(*args)

    return run


def solution(mesh):
    return build(mesh, XS, TGX)
```

```python
import functools
import math

import jax
import jax.numpy as jnp
import ml_dtypes
import numpy as np
from jax import lax
from jax.experimental import pallas as pl
from jax.experimental.pallas import tpu as pltpu
from jax.sharding import PartitionSpec as P

TGX = 8
XS = 4
LOSS_SCALE = 0.05
W = 128
F32 = jnp.float32
BF16 = jnp.bfloat16
MESH = pl.DeviceIdType.MESH


def table_parts():
    idx = np.arange(W)
    phase = (idx[:, None] * idx[None, :] % W) * (2.0 * math.pi / W)
    c, s = np.cos(phase) / math.sqrt(W), -np.sin(phase) / math.sqrt(W)
    left = np.block([[c, -s], [s, c]]).astype(np.float32)
    right = np.block([[c, s], [-s, c]]).astype(np.float32)

    def parts(m):
        hi = m.astype(ml_dtypes.bfloat16)
        return hi, (m - hi.astype(np.float32)).astype(ml_dtypes.bfloat16)

    lh, ll = parts(left)
    rh, rl = parts(right)
    by_rows = [np.concatenate([h, h, l], 0) for h, l in ((lh, ll), (rh, rl))]
    by_cols = [np.concatenate([h, l, h], 1) for h, l in ((lh, ll), (rh, rl))]
    return np.stack(by_rows), np.stack(by_cols)


def split(d):
    hi = d.astype(BF16)
    return hi, (d - hi.astype(F32)).astype(BF16)


def from_right(d, table):
    hi, lo = split(d)
    return jnp.dot(jnp.concatenate([hi, lo, hi], 1), table, preferred_element_type=F32)


def from_left(d, table):
    hi, lo = split(d)
    return jnp.dot(table, jnp.concatenate([hi, hi, lo], 0), preferred_element_type=F32)


def tree(terms):
    while len(terms) > 1:
        terms = [sum(terms[i + 1 : i + 2], terms[i]) for i in range(0, len(terms), 2)]
    return terms[0]


def swap_blocks(d):
    top = jnp.concatenate([d[:W, :W], d[W:, :W]], 1)
    low = jnp.concatenate([d[:W, W:], d[W:, W:]], 1)
    return jnp.concatenate([top, low], 0)


def kernel(
    geo,
    offs_ref, obj, probe, phase, meas, trow_h, tcol_h,
    out_g, out_p,
    ext, win, prb, hph, msr, trow, tcol, mid, offs, sel,
    gwin, gbuf, acc, low, r_right, r_low, fin,
    pg, p_core, s_core, p_x, s_x, p_y, p_z, tile,
    loc_sem, f1_s, f1_r, of_s, of_r, f2_s, f2_r, g1_s, g1_r, g2_s, g2_r, g3_s, g3_r,
    own_offs, pc_s, pc_r, px_s, px_r, py_s, py_r, pz_s, pz_r, qy_s, qy_r, qx_s, qx_r, qc_s, qc_r, beyond,
):
    X, Z, NB, tgx = geo
    T = X * Z * 2
    RC = W // NB
    XP = 2 * W // X
    YP = XP // NB
    half = NB // 2
    t = lax.axis_index("tile")
    j = lax.axis_index("batch")
    core = lax.rem(t, 2)
    z = lax.rem(t // 2, Z)
    x = t // (2 * Z)
    sib = t + 1 - 2 * core

    def z_tile(d):
        return (x * Z + lax.rem(z + d, Z)) * 2 + core

    def x_tile(d):
        return (lax.rem(x + d, X) * Z + z) * 2 + core

    def y_dev(d):
        return lax.rem(j + d, NB)

    def cls(dev):
        return 2 * lax.rem(dev, half) + dev // half

    def rows_of(dev):
        return pl.ds(pl.multiple_of(RC * cls(dev), RC), RC)

    near = (1, tgx, 1)
    reach = 4 if Z > 9 else Z - 1

    barrier = pltpu.get_barrier_semaphore()

    def greet(tile, dev):
        pl.semaphore_signal(barrier, inc=1, device_id=(tile, dev), device_id_type=MESH)

    for n in near[:2]:
        greet(lax.rem(t + n, T), j)
        greet(lax.rem(t + T - n, T), j)
    greet(sib, j)
    lax.fori_loop(1, NB, lambda d, c: (greet(t, y_dev(d)), c)[1], 0)
    lax.fori_loop(1, X, lambda d, c: (greet(x_tile(d), j), c)[1], 0)
    lax.fori_loop(1, reach + 1, lambda d, c: (greet(z_tile(d), j), c)[1], 0)
    more = reach if Z > 9 else 0
    lax.fori_loop(Z - more, Z, lambda d, c: (greet(z_tile(d), j), c)[1], 0)

    mine = rows_of(j)
    local = [
        pltpu.make_async_copy(obj.at[l, :, :, mine, :], ext.at[l, :, 0:2, :, 0 : 2 * W], loc_sem.at[l])
        for l in range(2)
    ] + [
        pltpu.make_async_copy(a, b, loc_sem.at[2 + i])
        for i, (a, b) in enumerate(((probe, prb), (phase, hph.at[0]), (meas, msr), (trow_h, trow), (tcol_h, tcol)))
    ]
    for c in local:
        c.start()

    c = pltpu.make_async_copy(offs_ref, own_offs, loc_sem.at[10])
    c.start()
    c.wait()
    row_off = own_offs[0]
    col_off = own_offs[1]
    offs[j, 0] = jnp.full((8, W), row_off, jnp.int32)
    offs[j, 1] = jnp.full((8, W), col_off, jnp.int32)

    pl.semaphore_wait(barrier, NB - 1 + X - 1 + reach + more + 5)
    for d in (reach, Z - reach) if more else ():
        pl.semaphore_signal(beyond, inc=1, device_id=(z_tile(d), j), device_id_type=MESH)

    def strip(l, i):
        n = near[i]
        src, dst = (
            (obj.at[l, :, :, mine, 0:W], ext.at[l, :, 0:2, :, 2 * W :]),
            (obj.at[l, :, 0, mine, :], ext.at[l, :, 2, :, 0 : 2 * W]),
            (ext.at[l, :, 2, :, 0:W], ext.at[l, :, 2, :, 2 * W :]),
        )[i]
        return pltpu.make_async_remote_copy(
            src, dst, f1_s.at[l, i], f1_r.at[l, i],
            device_id=(lax.rem(t + T - n, T), j), device_id_type=MESH,
        )

    def offs_copy(d):
        return pltpu.make_async_remote_copy(
            offs.at[j], offs.at[j], of_s.at[d - 1], of_r.at[d - 1],
            device_id=(t, y_dev(d)), device_id_type=MESH,
        )

    def offs_arrival(d):
        src = y_dev(NB - d)
        return pltpu.make_async_remote_copy(
            offs.at[src], offs.at[src], of_s.at[d - 1], of_r.at[d - 1],
            device_id=(t, src), device_id_type=MESH,
        )

    for i in (1, 0):
        strip(0, i).start()
    lax.fori_loop(1, NB, lambda d, c: (offs_copy(d).start(), c)[1], 0)
    for i in (1, 0):
        strip(1, i).start()

    for c in local[2:]:
        c.wait()
    ang = hph[0]
    hph[0] = jnp.cos(ang)
    hph[1] = jnp.sin(ang)
    r_in = jnp.bitwise_and(row_off, W - 1)
    c_in = jnp.bitwise_and(col_off, W - 1)
    for m in range(2):
        for q in range(2):
            v = prb[m, q * W : (q + 1) * W, :]
            prb[m, q * W : (q + 1) * W, :] = pltpu.roll(pltpu.roll(v, r_in, 0), c_in, 1)
    r_back = jnp.bitwise_and(W - r_in, W - 1)
    c_back = jnp.bitwise_and(W - c_in, W - 1)

    lanes = lax.broadcasted_iota(jnp.int32, (RC, W), 1)
    rows = lax.broadcasted_iota(jnp.int32, (RC, W), 0) + RC * cls(j)

    def masks(dev):
        ro = jnp.broadcast_to(offs[dev, 0, 0:1, :], (RC, W))
        co = jnp.broadcast_to(offs[dev, 1, 0:1, :], (RC, W))
        return (rows >= ro, rows >= ro - W), (lanes >= co, lanes >= co - W)

    def pick(m, a, b, c):
        return jnp.where(m[0], a, jnp.where(m[1], b, c))

    def selected(l, dev):
        rm, cm = masks(dev)
        out = []
        for q in range(2):
            part = [
                pick(cm, *(ext[l, q, b, :, k * W : (k + 1) * W] for k in range(3))) for b in range(3)
            ]
            out.append(pick(rm, *part))
        return out

    def f2_copy(l, d):
        return pltpu.make_async_remote_copy(
            sel.at[l, d - 1], win.at[l, :, mine, :], f2_s.at[l, d - 1], f2_r.at[l, d - 1],
            device_id=(t, y_dev(d)), device_id_type=MESH,
        )

    def f2_arrival(l, d):
        src = y_dev(NB - d)
        return pltpu.make_async_remote_copy(
            sel.at[l, d - 1], win.at[l, :, rows_of(src), :], f2_s.at[l, d - 1], f2_r.at[l, d - 1],
            device_id=(t, src), device_id_type=MESH,
        )

    def spread_window(l):
        def one(d, c):
            vals = selected(l, y_dev(d))
            for q in range(2):
                sel[l, d - 1, q] = vals[q]
            f2_copy(l, d).start()
            return c

        lax.fori_loop(1, NB, one, 0)
        vals = selected(l, j)
        for q in range(2):
            win[l, q, mine, :] = vals[q]

    for l in range(2):
        local[l].wait()
        strip(l, 1).wait_recv()
        strip(l, 2).start()
        for i in (0, 2):
            strip(l, i).wait_recv()
        if l == 0:
            lax.fori_loop(1, NB, lambda d, c: (offs_arrival(d).wait_recv(), c)[1], 0)
        spread_window(l)

    L, R = 0, 1

    def forward(d):
        return from_left(swap_blocks(from_right(d, trow[R])), tcol[L])

    def inverse(d):
        return from_right(swap_blocks(from_left(d, tcol[R])), trow[L])

    def forward_pr(d):
        return from_right(swap_blocks(from_left(d, tcol[L])), trow[R])

    def by_mode(blocks):
        return jnp.concatenate([jnp.concatenate(list(b), 1) for b in blocks], 0)

    def by_part(blocks):
        return jnp.concatenate(
            [jnp.concatenate([b[q] for b in blocks], 1) for q in range(2)], 0
        )

    def modes_of(d):
        return [(d[m * W : (m + 1) * W, :W], d[m * W : (m + 1) * W, W:]) for m in range(2)]

    def modes_of_pr(d):
        return [(d[:W, m * W : (m + 1) * W], d[W:, m * W : (m + 1) * W]) for m in range(2)]

    def mul(a, b):
        return a[0] * b[0] - a[1] * b[1], a[0] * b[1] + a[1] * b[0]

    def mul_conj(a, b):
        return a[0] * b[0] + a[1] * b[1], a[0] * b[1] - a[1] * b[0]

    def window(l):
        return win[l, 0], win[l, 1]

    def probe_mode(m):
        return prb[m, 0:W, :], prb[m, W:, :]

    def arrive_window(l):
        lax.fori_loop(1, NB, lambda d, c: (f2_arrival(l, d).wait_recv(), c)[1], 0)

    arrive_window(0)
    w0 = window(0)
    spec = forward(by_mode([mul(probe_mode(m), w0) for m in range(2)]))
    prop = (hph[0], hph[1])
    spec = by_part([mul(s, prop) for s in modes_of_pr(spec)])
    at1 = inverse(spec)
    mid[...] = at1
    arrive_window(1)
    w1 = window(1)
    far = forward(by_mode([mul(s, w1) for s in modes_of(at1)]))
    sq = far * far
    col = sq[:W, :] + sq[W:, :]
    err = (col[:, :W] + col[:, W:] - msr[...]) * (4.0 * LOSS_SCALE)
    err2 = jnp.concatenate([err, err], 1)
    back = inverse(far * jnp.concatenate([err2, err2], 0))
    gb = modes_of(back)
    ms = modes_of(mid[...])
    g1a, g1b = (mul_conj(ms[m], gb[m]) for m in range(2))
    gwin[1, 0] = g1a[0] + g1b[0]
    gwin[1, 1] = g1a[1] + g1b[1]

    def g1_copy(l, d):
        dev = y_dev(d)
        return pltpu.make_async_remote_copy(
            gwin.at[l, :, rows_of(dev), :], gbuf.at[j, l], g1_s.at[l, d - 1], g1_r.at[l, d - 1],
            device_id=(t, dev), device_id_type=MESH,
        )

    def g1_arrival(l, d):
        src = y_dev(NB - d)
        return pltpu.make_async_remote_copy(
            gwin.at[l, :, mine, :], gbuf.at[src, l], g1_s.at[l, d - 1], g1_r.at[l, d - 1],
            device_id=(t, src), device_id_type=MESH,
        )

    def spread_grad(l):
        lax.fori_loop(1, NB, lambda d, c: (g1_copy(l, d).start(), c)[1], 0)
        gbuf[j, l] = gwin[l, :, mine, :]

    spread_grad(1)
    w1 = window(1)
    spec = forward(by_mode([mul_conj(w1, g) for g in gb]))
    spec = by_part([mul_conj(prop, s) for s in modes_of_pr(spec)])
    gb = modes_of(inverse(spec))
    w0 = window(0)
    for m in range(2):
        gp = mul_conj(w0, gb[m])
        for q in range(2):
            pg[m, q * W : (q + 1) * W, :] = pltpu.roll(pltpu.roll(gp[q], c_back, 1), r_back, 0)
    core_copy = pltpu.make_async_remote_copy(
        pg.at[1 - core], p_core, pc_s, pc_r, device_id=(sib, j), device_id_type=MESH
    )
    core_copy.start()
    g0a, g0b = (mul_conj(probe_mode(m), gb[m]) for m in range(2))
    gwin[0, 0] = g0a[0] + g0b[0]
    gwin[0, 1] = g0a[1] + g0b[1]
    spread_grad(0)

    def px_rows(xx):
        return pl.ds(pl.multiple_of(XP * xx, XP), XP)

    def px_copy(d):
        xx = lax.rem(x + d, X)
        return pltpu.make_async_remote_copy(
            s_core.at[px_rows(xx)], p_x.at[d - 1], px_s.at[d - 1], px_r.at[d - 1],
            device_id=(x_tile(d), j), device_id_type=MESH,
        )

    def py_rows(yy):
        return pl.ds(pl.multiple_of(YP * yy, YP), YP)

    def py_copy(d):
        dev = y_dev(d)
        return pltpu.make_async_remote_copy(
            s_x.at[py_rows(dev)], p_y.at[d - 1], py_s.at[d - 1], py_r.at[d - 1],
            device_id=(t, dev), device_id_type=MESH,
        )

    def pz_copy(d):
        return pltpu.make_async_remote_copy(
            p_z.at[z], p_z.at[z], pz_s.at[d - 1], pz_r.at[d - 1],
            device_id=(z_tile(d), j), device_id_type=MESH,
        )

    def pz_arrival(d):
        zz = lax.rem(z + Z - d, Z)
        return pltpu.make_async_remote_copy(
            p_z.at[zz], p_z.at[zz], pz_s.at[d - 1], pz_r.at[d - 1],
            device_id=(z_tile(Z - d), j), device_id_type=MESH,
        )

    def out_rows(xx, yy):
        return pl.ds(pl.multiple_of(XP * xx + YP * yy, YP), YP)

    def qy_copy(d, arrival=False):
        own = y_dev(NB - d) if arrival else j
        return pltpu.make_async_remote_copy(
            tile, out_p.at[core, out_rows(x, own)], qy_s.at[d - 1], qy_r.at[d - 1],
            device_id=(t, y_dev(d)), device_id_type=MESH,
        )

    def qx_copy(d, arrival=False):
        own = lax.rem(x + X - d, X) if arrival else x
        piece = out_p.at[core, px_rows(own)]
        return pltpu.make_async_remote_copy(
            piece, piece, qx_s.at[d - 1], qx_r.at[d - 1],
            device_id=(x_tile(d), j), device_id_type=MESH,
        )

    def qc_copy(d, which):
        piece = out_p.at[which, px_rows(lax.rem(x + X - d, X))]
        return pltpu.make_async_remote_copy(
            piece, piece, qc_s.at[d], qc_r.at[d], device_id=(sib, j), device_id_type=MESH
        )

    core_copy.wait_recv()
    s_core[...] = pg[core] + p_core[...]
    for d in range(1, X):
        px_copy(d).start()

    def gather_grad(l):
        lax.fori_loop(1, NB, lambda d, c: (g1_arrival(l, d).wait_recv(), c)[1], 0)
        acc[l] = jnp.zeros(acc.shape[1:], F32)

        def one(dev, c):
            rm, cm = masks(dev)
            rsel = (rm[0], rm[1] & ~rm[0], ~rm[1])
            csel = (cm[0], cm[1] & ~cm[0], ~cm[1])
            for q in range(2):
                g = gbuf[dev, l, q]
                for b in range(3):
                    gr = jnp.where(rsel[b], g, 0.0)
                    for k in range(3):
                        at = (l, q, b, slice(None), slice(k * W, (k + 1) * W))
                        acc[at] = acc[at] + jnp.where(csel[k], gr, 0.0)
            return c

        lax.fori_loop(0, NB, one, 0)
        g2_copy(l, 0).start()

    def g2_copy(l, i):
        src, dst = ((acc.at[l, :, :, :, 2 * W :], r_right.at[l]), (low.at[l], r_low.at[l]))[i]
        return pltpu.make_async_remote_copy(
            src, dst, g2_s.at[l, i], g2_r.at[l, i],
            device_id=(lax.rem(t + near[i], T), j), device_id_type=MESH,
        )

    def pass_low(l):
        g2_copy(l, 0).wait_recv()
        for q in range(2):
            low[l, q, :, 0:W] = acc[l, q, 2, :, 0:W] + r_right[l, q, 2]
            low[l, q, :, W:] = acc[l, q, 2, :, W : 2 * W]
        g2_copy(l, 1).start()

    side = j // half

    def g_rows(which):
        return pl.ds(pl.multiple_of(RC * which, RC), RC)

    def g3_copy(l, which):
        return pltpu.make_async_remote_copy(
            fin.at[l, 1 - side], out_g.at[l, :, g_rows(which), :], g3_s.at[l], g3_r.at[l],
            device_id=(t, y_dev(half)), device_id_type=MESH,
        )

    def g_here(l):
        return pltpu.make_async_copy(fin.at[l, side], out_g.at[l, :, g_rows(side), :], loc_sem.at[7 + l])

    def join_grad(l):
        g2_copy(l, 1).wait_recv()
        for q in range(2):
            for b in range(2):
                one = acc[l, q, b, :, 0:W] + r_right[l, q, b]
                two = acc[l, q, b, :, W : 2 * W]
                if b == 0:
                    one = one + r_low[l, q, :, 0:W]
                    two = two + r_low[l, q, :, W:]
                fin[l, b, q, :, 0:W] = one
                fin[l, b, q, :, W:] = two
        g3_copy(l, side).start()
        g_here(l).start()

    def drain_early():
        for l in range(2):
            for i in range(3):
                strip(l, i).wait_send()

        def sent_y(d, c):
            offs_copy(d).wait_send()
            for l in range(2):
                f2_copy(l, d).wait_send()
                g1_copy(l, d).wait_send()
            py_copy(d).wait_send()
            return c

        lax.fori_loop(1, NB, sent_y, 0)
        for d in range(1, X):
            px_copy(d).wait_send()
        core_copy.wait_send()

    def drain_mid():
        for l in range(2):
            for i in range(2):
                g2_copy(l, i).wait_send()
        lax.fori_loop(1, Z, lambda d, c: (pz_copy(d).wait_send(), c)[1], 0)
        lax.fori_loop(1, NB, lambda d, c: (qy_copy(d).wait_send(), c)[1], 0)

    gather_grad(1)
    for d in range(1, X):
        px_copy(d).wait_recv()
    total = s_core[px_rows(x)]
    for d in range(1, X):
        total = total + p_x[d - 1]
    s_x[...] = total
    lax.fori_loop(1, NB, lambda d, c: (py_copy(d).start(), c)[1], 0)
    gather_grad(0)
    pass_low(1)
    lax.fori_loop(1, NB, lambda d, c: (py_copy(d).wait_recv(), c)[1], 0)
    p_z[z] = tree([s_x[py_rows(j)]] + [p_y[i] for i in range(NB - 1)])
    if more:
        pl.semaphore_wait(beyond, 2)
    lax.fori_loop(1, Z, lambda d, c: (pz_copy(d).start(), c)[1], 0)
    pass_low(0)
    join_grad(1)
    drain_early()
    lax.fori_loop(1, Z, lambda d, c: (pz_arrival(d).wait_recv(), c)[1], 0)
    tile[...] = tree([p_z[i] for i in range(Z)]) * (1.0 / (T * NB))
    lax.fori_loop(1, NB, lambda d, c: (qy_copy(d).start(), c)[1], 0)
    keep = pltpu.make_async_copy(tile, out_p.at[core, out_rows(x, j)], loc_sem.at[9])
    keep.start()
    join_grad(0)
    keep.wait()
    drain_mid()
    lax.fori_loop(1, NB, lambda d, c: (qy_copy(d, True).wait_recv(), c)[1], 0)
    for d in range(1, X):
        qx_copy(d).start()
    qc_copy(0, core).start()
    for d in range(1, X):
        qx_copy(d, True).wait_recv()
        qc_copy(d, core).start()

    for d in range(1, X):
        qx_copy(d).wait_send()
    for l in range(2):
        g_here(l).wait()
        g3_copy(l, side).wait_send()
        g3_copy(l, 1 - side).wait_recv()
    for d in range(X):
        qc_copy(d, core).wait_send()
    for d in range(X):
        qc_copy(d, 1 - core).wait_recv()


def local(geo, trow, tcol, object_slices, probe, prop_phase, scan_offsets, measured):
    X, Z, NB, _ = geo
    RC = W // NB
    XP = 2 * W // X
    YP = XP // NB
    dma = pltpu.SemaphoreType.DMA
    vm = pltpu.VMEM
    any_spec = pl.BlockSpec(memory_space=pltpu.HBM)
    scratch = [
        vm((2, 2, 3, RC, 3 * W), F32),
        vm((2, 2, W, W), F32),
        vm((2, 2 * W, W), F32),
        vm((2, W, W), F32),
        vm((W, W), F32),
        vm((2, 6 * W, 2 * W), BF16),
        vm((2, 2 * W, 6 * W), BF16),
        vm((2 * W, 2 * W), F32),
        vm((NB, 2, 8, W), jnp.int32),
        vm((2, NB - 1, 2, RC, W), F32),
        vm((2, 2, W, W), F32),
        vm((NB, 2, 2, RC, W), F32),
        vm((2, 2, 3, RC, 3 * W), F32),
        vm((2, 2, RC, 2 * W), F32),
        vm((2, 2, 3, RC, W), F32),
        vm((2, 2, RC, 2 * W), F32),
        vm((2, 2, 2, RC, 2 * W), F32),
        vm((2, 2 * W, W), F32),
        vm((2 * W, W), F32),
        vm((2 * W, W), F32),
        vm((X - 1, XP, W), F32),
        vm((XP, W), F32),
        vm((NB - 1, YP, W), F32),
        vm((Z, YP, W), F32),
        vm((YP, W), F32),
        dma((11,)),
        dma((2, 3)), dma((2, 3)), dma((NB - 1,)), dma((NB - 1,)),
        dma((2, NB - 1)), dma((2, NB - 1)), dma((2, NB - 1)), dma((2, NB - 1)),
        dma((2, 2)), dma((2, 2)), dma((2,)), dma((2,)),
        pltpu.SMEM((2,), jnp.int32), dma, dma, dma((X - 1,)), dma((X - 1,)), dma((NB - 1,)), dma((NB - 1,)),
        dma((max(Z - 1, 1),)), dma((max(Z - 1, 1),)), dma((NB - 1,)), dma((NB - 1,)),
        dma((X - 1,)), dma((X - 1,)), dma((X,)), dma((X,)), pltpu.SemaphoreType.REGULAR,
    ]
    grad, step = pl.pallas_call(
        functools.partial(kernel, geo),
        out_shape=(
            jax.ShapeDtypeStruct((2, 2, 2 * RC, 2 * W), F32),
            jax.ShapeDtypeStruct((2, 2 * W, W), F32),
        ),
        in_specs=[any_spec] * 7,
        out_specs=(any_spec, any_spec),
        scratch_shapes=scratch,
        compiler_params=pltpu.CompilerParams(
            collective_id=0, has_side_effects=True, vmem_limit_bytes=48 * 1024 * 1024
        ),
        name="ptycho",
    )(
        *(
            pltpu.with_memory_space_constraint(a, pltpu.HBM)
            for a in (
                scan_offsets.reshape(2),
                object_slices.reshape(2, 2, 2, W, 2 * W),
                probe.reshape(2, 2 * W, W),
                prop_phase,
                measured.reshape(W, W),
                trow,
                tcol,
            )
        ),
    )
    return grad[None], step.reshape(2, 2, W, W)


def build(mesh, xs, tgx):
    nb = mesh.shape["batch"]
    geo = (xs, mesh.shape["tile"] // (2 * xs), nb, tgx)
    by_rows, by_cols = table_parts()
    in_specs = (
        P("tile", None, None, None, None),
        P(),
        P(),
        P("tile", "batch", None),
        P("tile", "batch", None, None),
    )
    out_specs = (P("tile", None, None, "batch", None), P())

    def run(*args):
        body = functools.partial(local, geo, jnp.asarray(by_rows), jnp.asarray(by_cols))
        return jax.shard_map(body, mesh=mesh, in_specs=in_specs, out_specs=out_specs, check_vma=False)(*args)

    return run


def solution(mesh):
    return build(mesh, XS, TGX)
```

```python
import functools
import math

import jax
import jax.numpy as jnp
import ml_dtypes
import numpy as np
from jax import lax
from jax.experimental import pallas as pl
from jax.experimental.pallas import tpu as pltpu
from jax.sharding import PartitionSpec as P

TGX = 8
XS = 4
LOSS_SCALE = 0.05
W = 128
F32 = jnp.float32
BF16 = jnp.bfloat16
MESH = pl.DeviceIdType.MESH


def table_parts():
    idx = np.arange(W)
    phase = (idx[:, None] * idx[None, :] % W) * (2.0 * math.pi / W)
    c, s = np.cos(phase) / math.sqrt(W), -np.sin(phase) / math.sqrt(W)
    left = np.block([[c, -s], [s, c]]).astype(np.float32)
    right = np.block([[c, s], [-s, c]]).astype(np.float32)

    def parts(m):
        hi = m.astype(ml_dtypes.bfloat16)
        return hi, (m - hi.astype(np.float32)).astype(ml_dtypes.bfloat16)

    lh, ll = parts(left)
    rh, rl = parts(right)
    by_rows = [np.concatenate([h, h, l], 0) for h, l in ((lh, ll), (rh, rl))]
    by_cols = [np.concatenate([h, l, h], 1) for h, l in ((lh, ll), (rh, rl))]
    return np.stack(by_rows), np.stack(by_cols)


def split(d):
    hi = d.astype(BF16)
    return hi, (d - hi.astype(F32)).astype(BF16)


def from_right(d, table):
    hi, lo = split(d)
    return jnp.dot(jnp.concatenate([hi, lo, hi], 1), table, preferred_element_type=F32)


def from_left(d, table):
    hi, lo = split(d)
    return jnp.dot(table, jnp.concatenate([hi, hi, lo], 0), preferred_element_type=F32)


def tree(terms):
    while len(terms) > 1:
        terms = [sum(terms[i + 1 : i + 2], terms[i]) for i in range(0, len(terms), 2)]
    return terms[0]


def swap_blocks(d):
    top = jnp.concatenate([d[:W, :W], d[W:, :W]], 1)
    low = jnp.concatenate([d[:W, W:], d[W:, W:]], 1)
    return jnp.concatenate([top, low], 0)


def kernel(
    geo,
    offs_ref, obj, probe, phase, meas, trow_h, tcol_h,
    out_g, out_p,
    ext, win, prb, hph, msr, trow, tcol, mid, offs, sel,
    gwin, gbuf, acc, low, r_right, r_low, fin,
    pg, p_core, s_core, p_x, s_x, p_y, p_z, tile,
    loc_sem, f1_s, f1_r, of_s, of_r, f2_s, f2_r, g1_s, g1_r, g2_s, g2_r, g3_s, g3_r,
    own_offs, pc_s, pc_r, px_s, px_r, py_s, py_r, pz_s, pz_r, qy_s, qy_r, qx_s, qx_r, qc_s, qc_r, beyond,
):
    X, Z, NB, tgx = geo
    T = X * Z * 2
    RC = W // NB
    XP = 2 * W // X
    YP = XP // NB
    half = NB // 2
    t = lax.axis_index("tile")
    j = lax.axis_index("batch")
    core = lax.rem(t, 2)
    z = lax.rem(t // 2, Z)
    x = t // (2 * Z)
    sib = t + 1 - 2 * core

    def far_first(i, n):
        return n // 2 + (1 - 2 * lax.rem(i, 2)) * (i // 2)

    def z_tile(d):
        return (x * Z + lax.rem(z + d, Z)) * 2 + core

    def x_tile(d):
        return (lax.rem(x + d, X) * Z + z) * 2 + core

    def y_dev(d):
        return lax.rem(j + d, NB)

    def cls(dev):
        return 2 * lax.rem(dev, half) + dev // half

    def rows_of(dev):
        return pl.ds(pl.multiple_of(RC * cls(dev), RC), RC)

    near = (1, tgx, 1)
    reach = 4 if Z > 9 else Z - 1

    barrier = pltpu.get_barrier_semaphore()

    def greet(tile, dev):
        pl.semaphore_signal(barrier, inc=1, device_id=(tile, dev), device_id_type=MESH)

    for n in near[:2]:
        greet(lax.rem(t + n, T), j)
        greet(lax.rem(t + T - n, T), j)
    greet(sib, j)
    lax.fori_loop(1, NB, lambda d, c: (greet(t, y_dev(d)), c)[1], 0)
    lax.fori_loop(1, X, lambda d, c: (greet(x_tile(d), j), c)[1], 0)
    lax.fori_loop(1, reach + 1, lambda d, c: (greet(z_tile(d), j), c)[1], 0)
    more = reach if Z > 9 else 0
    lax.fori_loop(Z - more, Z, lambda d, c: (greet(z_tile(d), j), c)[1], 0)

    mine = rows_of(j)
    local = [
        pltpu.make_async_copy(obj.at[l, :, :, mine, :], ext.at[l, :, 0:2, :, 0 : 2 * W], loc_sem.at[l])
        for l in range(2)
    ] + [
        pltpu.make_async_copy(a, b, loc_sem.at[2 + i])
        for i, (a, b) in enumerate(((probe, prb), (phase, hph.at[0]), (meas, msr), (trow_h, trow), (tcol_h, tcol)))
    ]
    for c in local:
        c.start()

    c = pltpu.make_async_copy(offs_ref, own_offs, loc_sem.at[10])
    c.start()
    c.wait()
    row_off = own_offs[0]
    col_off = own_offs[1]
    offs[j, 0] = jnp.full((8, W), row_off, jnp.int32)
    offs[j, 1] = jnp.full((8, W), col_off, jnp.int32)

    pl.semaphore_wait(barrier, NB - 1 + X - 1 + reach + more + 5)
    for d in (reach, Z - reach) if more else ():
        pl.semaphore_signal(beyond, inc=1, device_id=(z_tile(d), j), device_id_type=MESH)

    def strip(l, i):
        n = near[i]
        src, dst = (
            (obj.at[l, :, :, mine, 0:W], ext.at[l, :, 0:2, :, 2 * W :]),
            (obj.at[l, :, 0, mine, :], ext.at[l, :, 2, :, 0 : 2 * W]),
            (ext.at[l, :, 2, :, 0:W], ext.at[l, :, 2, :, 2 * W :]),
        )[i]
        return pltpu.make_async_remote_copy(
            src, dst, f1_s.at[l, i], f1_r.at[l, i],
            device_id=(lax.rem(t + T - n, T), j), device_id_type=MESH,
        )

    def offs_copy(d):
        return pltpu.make_async_remote_copy(
            offs.at[j], offs.at[j], of_s.at[d - 1], of_r.at[d - 1],
            device_id=(t, y_dev(d)), device_id_type=MESH,
        )

    def offs_arrival(d):
        src = y_dev(NB - d)
        return pltpu.make_async_remote_copy(
            offs.at[src], offs.at[src], of_s.at[d - 1], of_r.at[d - 1],
            device_id=(t, src), device_id_type=MESH,
        )

    for i in (1, 0):
        strip(0, i).start()
    lax.fori_loop(1, NB, lambda d, c: (offs_copy(d).start(), c)[1], 0)
    for i in (1, 0):
        strip(1, i).start()

    for c in local[2:]:
        c.wait()
    ang = hph[0]
    hph[0] = jnp.cos(ang)
    hph[1] = jnp.sin(ang)
    r_in = jnp.bitwise_and(row_off, W - 1)
    c_in = jnp.bitwise_and(col_off, W - 1)
    for m in range(2):
        for q in range(2):
            v = prb[m, q * W : (q + 1) * W, :]
            prb[m, q * W : (q + 1) * W, :] = pltpu.roll(pltpu.roll(v, r_in, 0), c_in, 1)
    r_back = jnp.bitwise_and(W - r_in, W - 1)
    c_back = jnp.bitwise_and(W - c_in, W - 1)

    lanes = lax.broadcasted_iota(jnp.int32, (RC, W), 1)
    rows = lax.broadcasted_iota(jnp.int32, (RC, W), 0) + RC * cls(j)

    def masks(dev):
        ro = jnp.broadcast_to(offs[dev, 0, 0:1, :], (RC, W))
        co = jnp.broadcast_to(offs[dev, 1, 0:1, :], (RC, W))
        return (rows >= ro, rows >= ro - W), (lanes >= co, lanes >= co - W)

    def pick(m, a, b, c):
        return jnp.where(m[0], a, jnp.where(m[1], b, c))

    def selected(l, dev):
        rm, cm = masks(dev)
        out = []
        for q in range(2):
            part = [
                pick(cm, *(ext[l, q, b, :, k * W : (k + 1) * W] for k in range(3))) for b in range(3)
            ]
            out.append(pick(rm, *part))
        return out

    def f2_copy(l, d):
        return pltpu.make_async_remote_copy(
            sel.at[l, d - 1], win.at[l, :, mine, :], f2_s.at[l, d - 1], f2_r.at[l, d - 1],
            device_id=(t, y_dev(d)), device_id_type=MESH,
        )

    def f2_arrival(l, d):
        src = y_dev(NB - d)
        return pltpu.make_async_remote_copy(
            sel.at[l, d - 1], win.at[l, :, rows_of(src), :], f2_s.at[l, d - 1], f2_r.at[l, d - 1],
            device_id=(t, src), device_id_type=MESH,
        )

    def spread_window(l):
        def one(d, c):
            d = far_first(d, NB)
            vals = selected(l, y_dev(d))
            for q in range(2):
                sel[l, d - 1, q] = vals[q]
            f2_copy(l, d).start()
            return c

        lax.fori_loop(1, NB, one, 0)
        vals = selected(l, j)
        for q in range(2):
            win[l, q, mine, :] = vals[q]

    for l in range(2):
        local[l].wait()
        strip(l, 1).wait_recv()
        strip(l, 2).start()
        for i in (0, 2):
            strip(l, i).wait_recv()
        if l == 0:
            lax.fori_loop(1, NB, lambda d, c: (offs_arrival(d).wait_recv(), c)[1], 0)
        spread_window(l)

    L, R = 0, 1

    def forward(d):
        return from_left(swap_blocks(from_right(d, trow[R])), tcol[L])

    def inverse(d):
        return from_right(swap_blocks(from_left(d, tcol[R])), trow[L])

    def forward_pr(d):
        return from_right(swap_blocks(from_left(d, tcol[L])), trow[R])

    def by_mode(blocks):
        return jnp.concatenate([jnp.concatenate(list(b), 1) for b in blocks], 0)

    def by_part(blocks):
        return jnp.concatenate(
            [jnp.concatenate([b[q] for b in blocks], 1) for q in range(2)], 0
        )

    def modes_of(d):
        return [(d[m * W : (m + 1) * W, :W], d[m * W : (m + 1) * W, W:]) for m in range(2)]

    def modes_of_pr(d):
        return [(d[:W, m * W : (m + 1) * W], d[W:, m * W : (m + 1) * W]) for m in range(2)]

    def mul(a, b):
        return a[0] * b[0] - a[1] * b[1], a[0] * b[1] + a[1] * b[0]

    def mul_conj(a, b):
        return a[0] * b[0] + a[1] * b[1], a[0] * b[1] - a[1] * b[0]

    def window(l):
        return win[l, 0], win[l, 1]

    def probe_mode(m):
        return prb[m, 0:W, :], prb[m, W:, :]

    def arrive_window(l):
        lax.fori_loop(1, NB, lambda d, c: (f2_arrival(l, d).wait_recv(), c)[1], 0)

    arrive_window(0)
    w0 = window(0)
    spec = forward(by_mode([mul(probe_mode(m), w0) for m in range(2)]))
    prop = (hph[0], hph[1])
    spec = by_part([mul(s, prop) for s in modes_of_pr(spec)])
    at1 = inverse(spec)
    mid[...] = at1
    arrive_window(1)
    w1 = window(1)
    far = forward(by_mode([mul(s, w1) for s in modes_of(at1)]))
    sq = far * far
    col = sq[:W, :] + sq[W:, :]
    err = (col[:, :W] + col[:, W:] - msr[...]) * (4.0 * LOSS_SCALE)
    err2 = jnp.concatenate([err, err], 1)
    back = inverse(far * jnp.concatenate([err2, err2], 0))
    gb = modes_of(back)
    ms = modes_of(mid[...])
    g1a, g1b = (mul_conj(ms[m], gb[m]) for m in range(2))
    gwin[1, 0] = g1a[0] + g1b[0]
    gwin[1, 1] = g1a[1] + g1b[1]

    def g1_copy(l, d):
        dev = y_dev(d)
        return pltpu.make_async_remote_copy(
            gwin.at[l, :, rows_of(dev), :], gbuf.at[j, l], g1_s.at[l, d - 1], g1_r.at[l, d - 1],
            device_id=(t, dev), device_id_type=MESH,
        )

    def g1_arrival(l, d):
        src = y_dev(NB - d)
        return pltpu.make_async_remote_copy(
            gwin.at[l, :, mine, :], gbuf.at[src, l], g1_s.at[l, d - 1], g1_r.at[l, d - 1],
            device_id=(t, src), device_id_type=MESH,
        )

    def spread_grad(l):
        lax.fori_loop(1, NB, lambda d, c: (g1_copy(l, far_first(d, NB)).start(), c)[1], 0)
        gbuf[j, l] = gwin[l, :, mine, :]

    spread_grad(1)
    w1 = window(1)
    spec = forward(by_mode([mul_conj(w1, g) for g in gb]))
    spec = by_part([mul_conj(prop, s) for s in modes_of_pr(spec)])
    gb = modes_of(inverse(spec))
    w0 = window(0)
    for m in range(2):
        gp = mul_conj(w0, gb[m])
        for q in range(2):
            pg[m, q * W : (q + 1) * W, :] = pltpu.roll(pltpu.roll(gp[q], c_back, 1), r_back, 0)
    core_copy = pltpu.make_async_remote_copy(
        pg.at[1 - core], p_core, pc_s, pc_r, device_id=(sib, j), device_id_type=MESH
    )
    core_copy.start()
    g0a, g0b = (mul_conj(probe_mode(m), gb[m]) for m in range(2))
    gwin[0, 0] = g0a[0] + g0b[0]
    gwin[0, 1] = g0a[1] + g0b[1]
    spread_grad(0)

    def px_rows(xx):
        return pl.ds(pl.multiple_of(XP * xx, XP), XP)

    def px_copy(d):
        xx = lax.rem(x + d, X)
        return pltpu.make_async_remote_copy(
            s_core.at[px_rows(xx)], p_x.at[d - 1], px_s.at[d - 1], px_r.at[d - 1],
            device_id=(x_tile(d), j), device_id_type=MESH,
        )

    def py_rows(yy):
        return pl.ds(pl.multiple_of(YP * yy, YP), YP)

    def py_copy(d):
        dev = y_dev(d)
        return pltpu.make_async_remote_copy(
            s_x.at[py_rows(dev)], p_y.at[d - 1], py_s.at[d - 1], py_r.at[d - 1],
            device_id=(t, dev), device_id_type=MESH,
        )

    def pz_copy(d):
        return pltpu.make_async_remote_copy(
            p_z.at[z], p_z.at[z], pz_s.at[d - 1], pz_r.at[d - 1],
            device_id=(z_tile(d), j), device_id_type=MESH,
        )

    def pz_arrival(d):
        zz = lax.rem(z + Z - d, Z)
        return pltpu.make_async_remote_copy(
            p_z.at[zz], p_z.at[zz], pz_s.at[d - 1], pz_r.at[d - 1],
            device_id=(z_tile(Z - d), j), device_id_type=MESH,
        )

    def out_rows(xx, yy):
        return pl.ds(pl.multiple_of(XP * xx + YP * yy, YP), YP)

    def qy_copy(d, arrival=False):
        own = y_dev(NB - d) if arrival else j
        return pltpu.make_async_remote_copy(
            tile, out_p.at[core, out_rows(x, own)], qy_s.at[d - 1], qy_r.at[d - 1],
            device_id=(t, y_dev(d)), device_id_type=MESH,
        )

    def qx_copy(d, arrival=False):
        own = lax.rem(x + X - d, X) if arrival else x
        piece = out_p.at[core, px_rows(own)]
        return pltpu.make_async_remote_copy(
            piece, piece, qx_s.at[d - 1], qx_r.at[d - 1],
            device_id=(x_tile(d), j), device_id_type=MESH,
        )

    def qc_copy(d, which):
        piece = out_p.at[which, px_rows(lax.rem(x + X - d, X))]
        return pltpu.make_async_remote_copy(
            piece, piece, qc_s.at[d], qc_r.at[d], device_id=(sib, j), device_id_type=MESH
        )

    core_copy.wait_recv()
    s_core[...] = pg[core] + p_core[...]
    x_order = sorted(range(1, X), key=lambda d: -min(d, X - d))
    for d in x_order:
        px_copy(d).start()

    def gather_grad(l):
        lax.fori_loop(1, NB, lambda d, c: (g1_arrival(l, d).wait_recv(), c)[1], 0)
        acc[l] = jnp.zeros(acc.shape[1:], F32)

        def one(dev, c):
            rm, cm = masks(dev)
            rsel = (rm[0], rm[1] & ~rm[0], ~rm[1])
            csel = (cm[0], cm[1] & ~cm[0], ~cm[1])
            for q in range(2):
                g = gbuf[dev, l, q]
                for b in range(3):
                    gr = jnp.where(rsel[b], g, 0.0)
                    for k in range(3):
                        at = (l, q, b, slice(None), slice(k * W, (k + 1) * W))
                        acc[at] = acc[at] + jnp.where(csel[k], gr, 0.0)
            return c

        lax.fori_loop(0, NB, one, 0)
        g2_copy(l, 0).start()

    def g2_copy(l, i):
        src, dst = ((acc.at[l, :, :, :, 2 * W :], r_right.at[l]), (low.at[l], r_low.at[l]))[i]
        return pltpu.make_async_remote_copy(
            src, dst, g2_s.at[l, i], g2_r.at[l, i],
            device_id=(lax.rem(t + near[i], T), j), device_id_type=MESH,
        )

    def pass_low(l):
        g2_copy(l, 0).wait_recv()
        for q in range(2):
            low[l, q, :, 0:W] = acc[l, q, 2, :, 0:W] + r_right[l, q, 2]
            low[l, q, :, W:] = acc[l, q, 2, :, W : 2 * W]
        g2_copy(l, 1).start()

    side = j // half

    def g_rows(which):
        return pl.ds(pl.multiple_of(RC * which, RC), RC)

    def g3_copy(l, which):
        return pltpu.make_async_remote_copy(
            fin.at[l, 1 - side], out_g.at[l, :, g_rows(which), :], g3_s.at[l], g3_r.at[l],
            device_id=(t, y_dev(half)), device_id_type=MESH,
        )

    def g_here(l):
        return pltpu.make_async_copy(fin.at[l, side], out_g.at[l, :, g_rows(side), :], loc_sem.at[7 + l])

    def join_grad(l):
        g2_copy(l, 1).wait_recv()
        for q in range(2):
            for b in range(2):
                one = acc[l, q, b, :, 0:W] + r_right[l, q, b]
                two = acc[l, q, b, :, W : 2 * W]
                if b == 0:
                    one = one + r_low[l, q, :, 0:W]
                    two = two + r_low[l, q, :, W:]
                fin[l, b, q, :, 0:W] = one
                fin[l, b, q, :, W:] = two
        g3_copy(l, side).start()
        g_here(l).start()

    def drain_early():
        for l in range(2):
            for i in range(3):
                strip(l, i).wait_send()

        def sent_y(d, c):
            offs_copy(d).wait_send()
            for l in range(2):
                f2_copy(l, d).wait_send()
                g1_copy(l, d).wait_send()
            py_copy(d).wait_send()
            return c

        lax.fori_loop(1, NB, sent_y, 0)
        for d in range(1, X):
            px_copy(d).wait_send()
        core_copy.wait_send()

    def drain_mid():
        for l in range(2):
            for i in range(2):
                g2_copy(l, i).wait_send()
        lax.fori_loop(1, Z, lambda d, c: (pz_copy(d).wait_send(), c)[1], 0)
        lax.fori_loop(1, NB, lambda d, c: (qy_copy(d).wait_send(), c)[1], 0)

    gather_grad(1)
    for d in range(1, X):
        px_copy(d).wait_recv()
    total = s_core[px_rows(x)]
    for d in range(1, X):
        total = total + p_x[d - 1]
    s_x[...] = total
    lax.fori_loop(1, NB, lambda d, c: (py_copy(far_first(d, NB)).start(), c)[1], 0)
    gather_grad(0)
    pass_low(1)
    lax.fori_loop(1, NB, lambda d, c: (py_copy(d).wait_recv(), c)[1], 0)
    p_z[z] = tree([s_x[py_rows(j)]] + [p_y[i] for i in range(NB - 1)])
    if more:
        pl.semaphore_wait(beyond, 2)
    lax.fori_loop(1, Z, lambda d, c: (pz_copy(far_first(d, Z)).start(), c)[1], 0)
    pass_low(0)
    join_grad(1)
    drain_early()
    lax.fori_loop(1, Z, lambda d, c: (pz_arrival(d).wait_recv(), c)[1], 0)
    tile[...] = tree([p_z[i] for i in range(Z)]) * (1.0 / (T * NB))
    lax.fori_loop(1, NB, lambda d, c: (qy_copy(far_first(d, NB)).start(), c)[1], 0)
    keep = pltpu.make_async_copy(tile, out_p.at[core, out_rows(x, j)], loc_sem.at[9])
    keep.start()
    join_grad(0)
    keep.wait()
    drain_mid()
    lax.fori_loop(1, NB, lambda d, c: (qy_copy(d, True).wait_recv(), c)[1], 0)
    for d in x_order:
        qx_copy(d).start()
    qc_copy(0, core).start()
    for d in range(1, X):
        qx_copy(d, True).wait_recv()
        qc_copy(d, core).start()

    for d in range(1, X):
        qx_copy(d).wait_send()
    for l in range(2):
        g_here(l).wait()
        g3_copy(l, side).wait_send()
        g3_copy(l, 1 - side).wait_recv()
    for d in range(X):
        qc_copy(d, core).wait_send()
    for d in range(X):
        qc_copy(d, 1 - core).wait_recv()


def local(geo, trow, tcol, object_slices, probe, prop_phase, scan_offsets, measured):
    X, Z, NB, _ = geo
    RC = W // NB
    XP = 2 * W // X
    YP = XP // NB
    dma = pltpu.SemaphoreType.DMA
    vm = pltpu.VMEM
    any_spec = pl.BlockSpec(memory_space=pltpu.HBM)
    scratch = [
        vm((2, 2, 3, RC, 3 * W), F32),
        vm((2, 2, W, W), F32),
        vm((2, 2 * W, W), F32),
        vm((2, W, W), F32),
        vm((W, W), F32),
        vm((2, 6 * W, 2 * W), BF16),
        vm((2, 2 * W, 6 * W), BF16),
        vm((2 * W, 2 * W), F32),
        vm((NB, 2, 8, W), jnp.int32),
        vm((2, NB - 1, 2, RC, W), F32),
        vm((2, 2, W, W), F32),
        vm((NB, 2, 2, RC, W), F32),
        vm((2, 2, 3, RC, 3 * W), F32),
        vm((2, 2, RC, 2 * W), F32),
        vm((2, 2, 3, RC, W), F32),
        vm((2, 2, RC, 2 * W), F32),
        vm((2, 2, 2, RC, 2 * W), F32),
        vm((2, 2 * W, W), F32),
        vm((2 * W, W), F32),
        vm((2 * W, W), F32),
        vm((X - 1, XP, W), F32),
        vm((XP, W), F32),
        vm((NB - 1, YP, W), F32),
        vm((Z, YP, W), F32),
        vm((YP, W), F32),
        dma((11,)),
        dma((2, 3)), dma((2, 3)), dma((NB - 1,)), dma((NB - 1,)),
        dma((2, NB - 1)), dma((2, NB - 1)), dma((2, NB - 1)), dma((2, NB - 1)),
        dma((2, 2)), dma((2, 2)), dma((2,)), dma((2,)),
        pltpu.SMEM((2,), jnp.int32), dma, dma, dma((X - 1,)), dma((X - 1,)), dma((NB - 1,)), dma((NB - 1,)),
        dma((max(Z - 1, 1),)), dma((max(Z - 1, 1),)), dma((NB - 1,)), dma((NB - 1,)),
        dma((X - 1,)), dma((X - 1,)), dma((X,)), dma((X,)), pltpu.SemaphoreType.REGULAR,
    ]
    grad, step = pl.pallas_call(
        functools.partial(kernel, geo),
        out_shape=(
            jax.ShapeDtypeStruct((2, 2, 2 * RC, 2 * W), F32),
            jax.ShapeDtypeStruct((2, 2 * W, W), F32),
        ),
        in_specs=[any_spec] * 7,
        out_specs=(any_spec, any_spec),
        scratch_shapes=scratch,
        compiler_params=pltpu.CompilerParams(
            collective_id=0, has_side_effects=True, vmem_limit_bytes=48 * 1024 * 1024
        ),
        name="ptycho",
    )(
        *(
            pltpu.with_memory_space_constraint(a, pltpu.HBM)
            for a in (
                scan_offsets.reshape(2),
                object_slices.reshape(2, 2, 2, W, 2 * W),
                probe.reshape(2, 2 * W, W),
                prop_phase,
                measured.reshape(W, W),
                trow,
                tcol,
            )
        ),
    )
    return grad[None], step.reshape(2, 2, W, W)


def build(mesh, xs, tgx):
    nb = mesh.shape["batch"]
    geo = (xs, mesh.shape["tile"] // (2 * xs), nb, tgx)
    by_rows, by_cols = table_parts()
    in_specs = (
        P("tile", None, None, None, None),
        P(),
        P(),
        P("tile", "batch", None),
        P("tile", "batch", None, None),
    )
    out_specs = (P("tile", None, None, "batch", None), P())

    def run(*args):
        body = functools.partial(local, geo, jnp.asarray(by_rows), jnp.asarray(by_cols))
        return jax.shard_map(body, mesh=mesh, in_specs=in_specs, out_specs=out_specs, check_vma=False)(*args)

    return run


def solution(mesh):
    return build(mesh, XS, TGX)
```

```python
import functools
import math

import jax
import jax.numpy as jnp
import ml_dtypes
import numpy as np
from jax import lax
from jax.experimental import pallas as pl
from jax.experimental.pallas import tpu as pltpu
from jax.sharding import PartitionSpec as P

TGX = 8
XS = 4
LOSS_SCALE = 0.05
W = 128
F32 = jnp.float32
BF16 = jnp.bfloat16
MESH = pl.DeviceIdType.MESH


def table_parts():
    idx = np.arange(W)
    phase = (idx[:, None] * idx[None, :] % W) * (2.0 * math.pi / W)
    c, s = np.cos(phase) / math.sqrt(W), -np.sin(phase) / math.sqrt(W)
    left = np.block([[c, -s], [s, c]]).astype(np.float32)
    right = np.block([[c, s], [-s, c]]).astype(np.float32)

    def parts(m):
        hi = m.astype(ml_dtypes.bfloat16)
        return hi, (m - hi.astype(np.float32)).astype(ml_dtypes.bfloat16)

    lh, ll = parts(left)
    rh, rl = parts(right)
    by_rows = [np.concatenate([h, h, l], 0) for h, l in ((lh, ll), (rh, rl))]
    by_cols = [np.concatenate([h, l, h], 1) for h, l in ((lh, ll), (rh, rl))]
    return np.stack(by_rows), np.stack(by_cols)


def split(d):
    hi = d.astype(BF16)
    return hi, (d - hi.astype(F32)).astype(BF16)


def from_right(d, table):
    hi, lo = split(d)
    return jnp.dot(jnp.concatenate([hi, lo, hi], 1), table, preferred_element_type=F32)


def from_left(d, table):
    hi, lo = split(d)
    return jnp.dot(table, jnp.concatenate([hi, hi, lo], 0), preferred_element_type=F32)


def tree(terms):
    while len(terms) > 1:
        terms = [sum(terms[i + 1 : i + 2], terms[i]) for i in range(0, len(terms), 2)]
    return terms[0]


def swap_blocks(d):
    top = jnp.concatenate([d[:W, :W], d[W:, :W]], 1)
    low = jnp.concatenate([d[:W, W:], d[W:, W:]], 1)
    return jnp.concatenate([top, low], 0)


def kernel(
    geo,
    offs_ref, obj, probe, phase, meas, trow_h, tcol_h,
    out_g, out_p,
    ext, win, prb, hph, msr, trow, tcol, mid, offs, sel,
    gwin, gbuf, acc, low, r_right, r_low, fin,
    pg, p_core, s_core, p_x, s_x, p_y, p_z, tile,
    loc_sem, f1_s, f1_r, of_s, of_r, f2_s, f2_r, g1_s, g1_r, g2_s, g2_r, g3_s, g3_r,
    own_offs, pc_s, pc_r, px_s, px_r, py_s, py_r, pz_s, pz_r, qy_s, qy_r, qx_s, qx_r, qc_s, qc_r, beyond,
):
    X, Z, NB, tgx = geo
    T = X * Z * 2
    RC = W // NB
    XP = 2 * W // X
    YP = XP // NB
    half = NB // 2
    t = lax.axis_index("tile")
    j = lax.axis_index("batch")
    core = lax.rem(t, 2)
    z = lax.rem(t // 2, Z)
    x = t // (2 * Z)
    sib = t + 1 - 2 * core

    def far_first(i, n):
        return n // 2 + (1 - 2 * lax.rem(i, 2)) * (i // 2)

    def z_tile(d):
        return (x * Z + lax.rem(z + d, Z)) * 2 + core

    def x_tile(d):
        return (lax.rem(x + d, X) * Z + z) * 2 + core

    def y_dev(d):
        return lax.rem(j + d, NB)

    def cls(dev):
        return 2 * lax.rem(dev, half) + dev // half

    def rows_of(dev):
        return pl.ds(pl.multiple_of(RC * cls(dev), RC), RC)

    near = (1, tgx, 1)
    reach = 4 if Z > 9 else Z - 1

    barrier = pltpu.get_barrier_semaphore()

    def greet(tile, dev):
        pl.semaphore_signal(barrier, inc=1, device_id=(tile, dev), device_id_type=MESH)

    for n in near[:2]:
        greet(lax.rem(t + n, T), j)
        greet(lax.rem(t + T - n, T), j)
    greet(sib, j)
    lax.fori_loop(1, NB, lambda d, c: (greet(t, y_dev(far_first(d, NB))), c)[1], 0)
    lax.fori_loop(1, X, lambda d, c: (greet(x_tile(d), j), c)[1], 0)
    lax.fori_loop(1, reach + 1, lambda d, c: (greet(z_tile(d), j), c)[1], 0)
    more = reach if Z > 9 else 0
    lax.fori_loop(Z - more, Z, lambda d, c: (greet(z_tile(d), j), c)[1], 0)

    mine = rows_of(j)
    local = [
        pltpu.make_async_copy(obj.at[l, :, :, mine, :], ext.at[l, :, 0:2, :, 0 : 2 * W], loc_sem.at[l])
        for l in range(2)
    ] + [
        pltpu.make_async_copy(a, b, loc_sem.at[2 + i])
        for i, (a, b) in enumerate(((probe, prb), (phase, hph.at[0]), (meas, msr), (trow_h, trow), (tcol_h, tcol)))
    ]
    for c in local:
        c.start()

    c = pltpu.make_async_copy(offs_ref, own_offs, loc_sem.at[10])
    c.start()
    c.wait()
    row_off = own_offs[0]
    col_off = own_offs[1]
    offs[j, 0] = jnp.full((8, W), row_off, jnp.int32)
    offs[j, 1] = jnp.full((8, W), col_off, jnp.int32)

    pl.semaphore_wait(barrier, NB - 1 + X - 1 + reach + more + 5)
    for d in (reach, Z - reach) if more else ():
        pl.semaphore_signal(beyond, inc=1, device_id=(z_tile(d), j), device_id_type=MESH)

    def strip(l, i):
        n = near[i]
        src, dst = (
            (obj.at[l, :, :, mine, 0:W], ext.at[l, :, 0:2, :, 2 * W :]),
            (obj.at[l, :, 0, mine, :], ext.at[l, :, 2, :, 0 : 2 * W]),
            (ext.at[l, :, 2, :, 0:W], ext.at[l, :, 2, :, 2 * W :]),
        )[i]
        return pltpu.make_async_remote_copy(
            src, dst, f1_s.at[l, i], f1_r.at[l, i],
            device_id=(lax.rem(t + T - n, T), j), device_id_type=MESH,
        )

    def offs_copy(d):
        return pltpu.make_async_remote_copy(
            offs.at[j], offs.at[j], of_s.at[d - 1], of_r.at[d - 1],
            device_id=(t, y_dev(d)), device_id_type=MESH,
        )

    def offs_arrival(d):
        src = y_dev(NB - d)
        return pltpu.make_async_remote_copy(
            offs.at[src], offs.at[src], of_s.at[d - 1], of_r.at[d - 1],
            device_id=(t, src), device_id_type=MESH,
        )

    for i in (1, 0):
        strip(0, i).start()
    lax.fori_loop(1, NB, lambda d, c: (offs_copy(far_first(d, NB)).start(), c)[1], 0)
    for i in (1, 0):
        strip(1, i).start()

    for c in local[2:]:
        c.wait()
    ang = hph[0]
    hph[0] = jnp.cos(ang)
    hph[1] = jnp.sin(ang)
    r_in = jnp.bitwise_and(row_off, W - 1)
    c_in = jnp.bitwise_and(col_off, W - 1)
    for m in range(2):
        for q in range(2):
            v = prb[m, q * W : (q + 1) * W, :]
            prb[m, q * W : (q + 1) * W, :] = pltpu.roll(pltpu.roll(v, r_in, 0), c_in, 1)
    r_back = jnp.bitwise_and(W - r_in, W - 1)
    c_back = jnp.bitwise_and(W - c_in, W - 1)

    lanes = lax.broadcasted_iota(jnp.int32, (RC, W), 1)
    rows = lax.broadcasted_iota(jnp.int32, (RC, W), 0) + RC * cls(j)

    def masks(dev):
        ro = jnp.broadcast_to(offs[dev, 0, 0:1, :], (RC, W))
        co = jnp.broadcast_to(offs[dev, 1, 0:1, :], (RC, W))
        return (rows >= ro, rows >= ro - W), (lanes >= co, lanes >= co - W)

    def pick(m, a, b, c):
        return jnp.where(m[0], a, jnp.where(m[1], b, c))

    def selected(l, dev):
        rm, cm = masks(dev)
        out = []
        for q in range(2):
            part = [
                pick(cm, *(ext[l, q, b, :, k * W : (k + 1) * W] for k in range(3))) for b in range(3)
            ]
            out.append(pick(rm, *part))
        return out

    def f2_copy(l, d):
        return pltpu.make_async_remote_copy(
            sel.at[l, d - 1], win.at[l, :, mine, :], f2_s.at[l, d - 1], f2_r.at[l, d - 1],
            device_id=(t, y_dev(d)), device_id_type=MESH,
        )

    def f2_arrival(l, d):
        src = y_dev(NB - d)
        return pltpu.make_async_remote_copy(
            sel.at[l, d - 1], win.at[l, :, rows_of(src), :], f2_s.at[l, d - 1], f2_r.at[l, d - 1],
            device_id=(t, src), device_id_type=MESH,
        )

    def spread_window(l):
        def one(d, c):
            d = far_first(d, NB)
            vals = selected(l, y_dev(d))
            for q in range(2):
                sel[l, d - 1, q] = vals[q]
            f2_copy(l, d).start()
            return c

        lax.fori_loop(1, NB, one, 0)
        vals = selected(l, j)
        for q in range(2):
            win[l, q, mine, :] = vals[q]

    for l in range(2):
        local[l].wait()
        strip(l, 1).wait_recv()
        strip(l, 2).start()
        for i in (0, 2):
            strip(l, i).wait_recv()
        if l == 0:
            lax.fori_loop(1, NB, lambda d, c: (offs_arrival(d).wait_recv(), c)[1], 0)
        spread_window(l)

    L, R = 0, 1

    def forward(d):
        return from_left(swap_blocks(from_right(d, trow[R])), tcol[L])

    def inverse(d):
        return from_right(swap_blocks(from_left(d, tcol[R])), trow[L])

    def forward_pr(d):
        return from_right(swap_blocks(from_left(d, tcol[L])), trow[R])

    def by_mode(blocks):
        return jnp.concatenate([jnp.concatenate(list(b), 1) for b in blocks], 0)

    def by_part(blocks):
        return jnp.concatenate(
            [jnp.concatenate([b[q] for b in blocks], 1) for q in range(2)], 0
        )

    def modes_of(d):
        return [(d[m * W : (m + 1) * W, :W], d[m * W : (m + 1) * W, W:]) for m in range(2)]

    def modes_of_pr(d):
        return [(d[:W, m * W : (m + 1) * W], d[W:, m * W : (m + 1) * W]) for m in range(2)]

    def mul(a, b):
        return a[0] * b[0] - a[1] * b[1], a[0] * b[1] + a[1] * b[0]

    def mul_conj(a, b):
        return a[0] * b[0] + a[1] * b[1], a[0] * b[1] - a[1] * b[0]

    def window(l):
        return win[l, 0], win[l, 1]

    def probe_mode(m):
        return prb[m, 0:W, :], prb[m, W:, :]

    def arrive_window(l):
        lax.fori_loop(1, NB, lambda d, c: (f2_arrival(l, d).wait_recv(), c)[1], 0)

    arrive_window(0)
    w0 = window(0)
    spec = forward(by_mode([mul(probe_mode(m), w0) for m in range(2)]))
    prop = (hph[0], hph[1])
    spec = by_part([mul(s, prop) for s in modes_of_pr(spec)])
    at1 = inverse(spec)
    mid[...] = at1
    arrive_window(1)
    w1 = window(1)
    far = forward(by_mode([mul(s, w1) for s in modes_of(at1)]))
    sq = far * far
    col = sq[:W, :] + sq[W:, :]
    err = (col[:, :W] + col[:, W:] - msr[...]) * (4.0 * LOSS_SCALE)
    err2 = jnp.concatenate([err, err], 1)
    back = inverse(far * jnp.concatenate([err2, err2], 0))
    gb = modes_of(back)
    ms = modes_of(mid[...])
    g1a, g1b = (mul_conj(ms[m], gb[m]) for m in range(2))
    gwin[1, 0] = g1a[0] + g1b[0]
    gwin[1, 1] = g1a[1] + g1b[1]

    def g1_copy(l, d):
        dev = y_dev(d)
        return pltpu.make_async_remote_copy(
            gwin.at[l, :, rows_of(dev), :], gbuf.at[j, l], g1_s.at[l, d - 1], g1_r.at[l, d - 1],
            device_id=(t, dev), device_id_type=MESH,
        )

    def g1_arrival(l, d):
        src = y_dev(NB - d)
        return pltpu.make_async_remote_copy(
            gwin.at[l, :, mine, :], gbuf.at[src, l], g1_s.at[l, d - 1], g1_r.at[l, d - 1],
            device_id=(t, src), device_id_type=MESH,
        )

    def spread_grad(l):
        lax.fori_loop(1, NB, lambda d, c: (g1_copy(l, far_first(d, NB)).start(), c)[1], 0)
        gbuf[j, l] = gwin[l, :, mine, :]

    spread_grad(1)
    w1 = window(1)
    spec = forward(by_mode([mul_conj(w1, g) for g in gb]))
    spec = by_part([mul_conj(prop, s) for s in modes_of_pr(spec)])
    gb = modes_of(inverse(spec))
    g0a, g0b = (mul_conj(probe_mode(m), gb[m]) for m in range(2))
    gwin[0, 0] = g0a[0] + g0b[0]
    gwin[0, 1] = g0a[1] + g0b[1]
    spread_grad(0)
    w0 = window(0)
    for m in range(2):
        gp = mul_conj(w0, gb[m])
        for q in range(2):
            pg[m, q * W : (q + 1) * W, :] = pltpu.roll(pltpu.roll(gp[q], c_back, 1), r_back, 0)
    core_copy = pltpu.make_async_remote_copy(
        pg.at[1 - core], p_core, pc_s, pc_r, device_id=(sib, j), device_id_type=MESH
    )
    core_copy.start()

    def px_rows(xx):
        return pl.ds(pl.multiple_of(XP * xx, XP), XP)

    def px_copy(d):
        xx = lax.rem(x + d, X)
        return pltpu.make_async_remote_copy(
            s_core.at[px_rows(xx)], p_x.at[d - 1], px_s.at[d - 1], px_r.at[d - 1],
            device_id=(x_tile(d), j), device_id_type=MESH,
        )

    def py_rows(yy):
        return pl.ds(pl.multiple_of(YP * yy, YP), YP)

    def py_copy(d):
        dev = y_dev(d)
        return pltpu.make_async_remote_copy(
            s_x.at[py_rows(dev)], p_y.at[d - 1], py_s.at[d - 1], py_r.at[d - 1],
            device_id=(t, dev), device_id_type=MESH,
        )

    def pz_copy(d):
        return pltpu.make_async_remote_copy(
            p_z.at[z], p_z.at[z], pz_s.at[d - 1], pz_r.at[d - 1],
            device_id=(z_tile(d), j), device_id_type=MESH,
        )

    def pz_arrival(d):
        zz = lax.rem(z + Z - d, Z)
        return pltpu.make_async_remote_copy(
            p_z.at[zz], p_z.at[zz], pz_s.at[d - 1], pz_r.at[d - 1],
            device_id=(z_tile(Z - d), j), device_id_type=MESH,
        )

    def out_rows(xx, yy):
        return pl.ds(pl.multiple_of(XP * xx + YP * yy, YP), YP)

    def qy_copy(d, arrival=False):
        own = y_dev(NB - d) if arrival else j
        return pltpu.make_async_remote_copy(
            tile, out_p.at[core, out_rows(x, own)], qy_s.at[d - 1], qy_r.at[d - 1],
            device_id=(t, y_dev(d)), device_id_type=MESH,
        )

    def qx_copy(d, arrival=False):
        own = lax.rem(x + X - d, X) if arrival else x
        piece = out_p.at[core, px_rows(own)]
        return pltpu.make_async_remote_copy(
            piece, piece, qx_s.at[d - 1], qx_r.at[d - 1],
            device_id=(x_tile(d), j), device_id_type=MESH,
        )

    def qc_copy(d, which):
        piece = out_p.at[which, px_rows(lax.rem(x + X - d, X))]
        return pltpu.make_async_remote_copy(
            piece, piece, qc_s.at[d], qc_r.at[d], device_id=(sib, j), device_id_type=MESH
        )

    core_copy.wait_recv()
    s_core[...] = pg[core] + p_core[...]
    x_order = sorted(range(1, X), key=lambda d: -min(d, X - d))
    for d in x_order:
        px_copy(d).start()

    def gather_grad(l):
        lax.fori_loop(1, NB, lambda d, c: (g1_arrival(l, d).wait_recv(), c)[1], 0)
        acc[l] = jnp.zeros(acc.shape[1:], F32)

        def one(dev, c):
            rm, cm = masks(dev)
            rsel = (rm[0], rm[1] & ~rm[0], ~rm[1])
            csel = (cm[0], cm[1] & ~cm[0], ~cm[1])
            for q in range(2):
                g = gbuf[dev, l, q]
                for b in range(3):
                    gr = jnp.where(rsel[b], g, 0.0)
                    for k in range(3):
                        at = (l, q, b, slice(None), slice(k * W, (k + 1) * W))
                        acc[at] = acc[at] + jnp.where(csel[k], gr, 0.0)
            return c

        lax.fori_loop(0, NB, one, 0)
        g2_copy(l, 0).start()

    def g2_copy(l, i):
        src, dst = ((acc.at[l, :, :, :, 2 * W :], r_right.at[l]), (low.at[l], r_low.at[l]))[i]
        return pltpu.make_async_remote_copy(
            src, dst, g2_s.at[l, i], g2_r.at[l, i],
            device_id=(lax.rem(t + near[i], T), j), device_id_type=MESH,
        )

    def pass_low(l):
        g2_copy(l, 0).wait_recv()
        for q in range(2):
            low[l, q, :, 0:W] = acc[l, q, 2, :, 0:W] + r_right[l, q, 2]
            low[l, q, :, W:] = acc[l, q, 2, :, W : 2 * W]
        g2_copy(l, 1).start()

    side = j // half

    def g_rows(which):
        return pl.ds(pl.multiple_of(RC * which, RC), RC)

    def g3_copy(l, which):
        return pltpu.make_async_remote_copy(
            fin.at[l, 1 - side], out_g.at[l, :, g_rows(which), :], g3_s.at[l], g3_r.at[l],
            device_id=(t, y_dev(half)), device_id_type=MESH,
        )

    def g_here(l):
        return pltpu.make_async_copy(fin.at[l, side], out_g.at[l, :, g_rows(side), :], loc_sem.at[7 + l])

    def join_grad(l):
        g2_copy(l, 1).wait_recv()
        for q in range(2):
            for b in range(2):
                one = acc[l, q, b, :, 0:W] + r_right[l, q, b]
                two = acc[l, q, b, :, W : 2 * W]
                if b == 0:
                    one = one + r_low[l, q, :, 0:W]
                    two = two + r_low[l, q, :, W:]
                fin[l, b, q, :, 0:W] = one
                fin[l, b, q, :, W:] = two
        g3_copy(l, side).start()
        g_here(l).start()

    def drain_early():
        for l in range(2):
            for i in range(3):
                strip(l, i).wait_send()

        def sent_y(d, c):
            offs_copy(d).wait_send()
            for l in range(2):
                f2_copy(l, d).wait_send()
                g1_copy(l, d).wait_send()
            py_copy(d).wait_send()
            return c

        lax.fori_loop(1, NB, sent_y, 0)
        for d in range(1, X):
            px_copy(d).wait_send()
        core_copy.wait_send()

    def drain_mid():
        for l in range(2):
            for i in range(2):
                g2_copy(l, i).wait_send()
        lax.fori_loop(1, Z, lambda d, c: (pz_copy(d).wait_send(), c)[1], 0)
        lax.fori_loop(1, NB, lambda d, c: (qy_copy(d).wait_send(), c)[1], 0)

    gather_grad(1)
    for d in range(1, X):
        px_copy(d).wait_recv()
    total = s_core[px_rows(x)]
    for d in range(1, X):
        total = total + p_x[d - 1]
    s_x[...] = total
    lax.fori_loop(1, NB, lambda d, c: (py_copy(far_first(d, NB)).start(), c)[1], 0)
    gather_grad(0)
    pass_low(1)
    lax.fori_loop(1, NB, lambda d, c: (py_copy(d).wait_recv(), c)[1], 0)
    p_z[z] = tree([s_x[py_rows(j)]] + [p_y[i] for i in range(NB - 1)])
    if more:
        pl.semaphore_wait(beyond, 2)
    lax.fori_loop(1, Z, lambda d, c: (pz_copy(far_first(d, Z)).start(), c)[1], 0)
    pass_low(0)
    join_grad(1)
    drain_early()
    lax.fori_loop(1, Z, lambda d, c: (pz_arrival(d).wait_recv(), c)[1], 0)
    tile[...] = tree([p_z[i] for i in range(Z)]) * (1.0 / (T * NB))
    lax.fori_loop(1, NB, lambda d, c: (qy_copy(far_first(d, NB)).start(), c)[1], 0)
    keep = pltpu.make_async_copy(tile, out_p.at[core, out_rows(x, j)], loc_sem.at[9])
    keep.start()
    join_grad(0)
    keep.wait()
    drain_mid()
    lax.fori_loop(1, NB, lambda d, c: (qy_copy(d, True).wait_recv(), c)[1], 0)
    for d in x_order:
        qx_copy(d).start()
    qc_copy(0, core).start()
    for d in range(1, X):
        qx_copy(d, True).wait_recv()
        qc_copy(d, core).start()

    for d in range(1, X):
        qx_copy(d).wait_send()
    for l in range(2):
        g_here(l).wait()
        g3_copy(l, side).wait_send()
        g3_copy(l, 1 - side).wait_recv()
    for d in range(X):
        qc_copy(d, core).wait_send()
    for d in range(X):
        qc_copy(d, 1 - core).wait_recv()


def local(geo, trow, tcol, object_slices, probe, prop_phase, scan_offsets, measured):
    X, Z, NB, _ = geo
    RC = W // NB
    XP = 2 * W // X
    YP = XP // NB
    dma = pltpu.SemaphoreType.DMA
    vm = pltpu.VMEM
    any_spec = pl.BlockSpec(memory_space=pltpu.HBM)
    scratch = [
        vm((2, 2, 3, RC, 3 * W), F32),
        vm((2, 2, W, W), F32),
        vm((2, 2 * W, W), F32),
        vm((2, W, W), F32),
        vm((W, W), F32),
        vm((2, 6 * W, 2 * W), BF16),
        vm((2, 2 * W, 6 * W), BF16),
        vm((2 * W, 2 * W), F32),
        vm((NB, 2, 8, W), jnp.int32),
        vm((2, NB - 1, 2, RC, W), F32),
        vm((2, 2, W, W), F32),
        vm((NB, 2, 2, RC, W), F32),
        vm((2, 2, 3, RC, 3 * W), F32),
        vm((2, 2, RC, 2 * W), F32),
        vm((2, 2, 3, RC, W), F32),
        vm((2, 2, RC, 2 * W), F32),
        vm((2, 2, 2, RC, 2 * W), F32),
        vm((2, 2 * W, W), F32),
        vm((2 * W, W), F32),
        vm((2 * W, W), F32),
        vm((X - 1, XP, W), F32),
        vm((XP, W), F32),
        vm((NB - 1, YP, W), F32),
        vm((Z, YP, W), F32),
        vm((YP, W), F32),
        dma((11,)),
        dma((2, 3)), dma((2, 3)), dma((NB - 1,)), dma((NB - 1,)),
        dma((2, NB - 1)), dma((2, NB - 1)), dma((2, NB - 1)), dma((2, NB - 1)),
        dma((2, 2)), dma((2, 2)), dma((2,)), dma((2,)),
        pltpu.SMEM((2,), jnp.int32), dma, dma, dma((X - 1,)), dma((X - 1,)), dma((NB - 1,)), dma((NB - 1,)),
        dma((max(Z - 1, 1),)), dma((max(Z - 1, 1),)), dma((NB - 1,)), dma((NB - 1,)),
        dma((X - 1,)), dma((X - 1,)), dma((X,)), dma((X,)), pltpu.SemaphoreType.REGULAR,
    ]
    grad, step = pl.pallas_call(
        functools.partial(kernel, geo),
        out_shape=(
            jax.ShapeDtypeStruct((2, 2, 2 * RC, 2 * W), F32),
            jax.ShapeDtypeStruct((2, 2 * W, W), F32),
        ),
        in_specs=[any_spec] * 7,
        out_specs=(any_spec, any_spec),
        scratch_shapes=scratch,
        compiler_params=pltpu.CompilerParams(
            collective_id=0, has_side_effects=True, vmem_limit_bytes=48 * 1024 * 1024
        ),
        name="ptycho",
    )(
        *(
            pltpu.with_memory_space_constraint(a, pltpu.HBM)
            for a in (
                scan_offsets.reshape(2),
                object_slices.reshape(2, 2, 2, W, 2 * W),
                probe.reshape(2, 2 * W, W),
                prop_phase,
                measured.reshape(W, W),
                trow,
                tcol,
            )
        ),
    )
    return grad[None], step.reshape(2, 2, W, W)


def build(mesh, xs, tgx):
    nb = mesh.shape["batch"]
    geo = (xs, mesh.shape["tile"] // (2 * xs), nb, tgx)
    by_rows, by_cols = table_parts()
    in_specs = (
        P("tile", None, None, None, None),
        P(),
        P(),
        P("tile", "batch", None),
        P("tile", "batch", None, None),
    )
    out_specs = (P("tile", None, None, "batch", None), P())

    def run(*args):
        body = functools.partial(local, geo, jnp.asarray(by_rows), jnp.asarray(by_cols))
        return jax.shard_map(body, mesh=mesh, in_specs=in_specs, out_specs=out_specs, check_vma=False)(*args)

    return run


def solution(mesh):
    return build(mesh, XS, TGX)
```
